128 devices in a mesh: rows: 32 (over x, z, core), cols: 4 (over y).
Axes of the slice: x: 4, y: 4, z: 4, core: 2. Of those that a mesh axis runs over, the one named last changes fastest.
Arguments:
- conc: float32 [8, 48, 256, 512], P(None, None, 'rows', 'cols'), may hold values from 0 to 2
- nwp: bfloat16 [2, 137, 65536], P(None, None, 'rows'), may hold values from -0.3 to 0.3
- lev_lo: int32 [48], replicated, may hold values from 0 to 135
- frac: float32 [48], replicated, may hold values from 0 to 1
- pick: int32 [32, 4, 32, 64], P('rows', 'cols'), may hold values from 0 to 2047
- corner_slot: int32 [4, 256, 512], P(None, 'rows', 'cols'), may hold values from 0 to 2047
- corner_wt: float32 [4, 256, 512], P(None, 'rows', 'cols'), may hold values from 0.25 to 1
- settle: float32 [8], replicated, may hold values from 0.015 to 0.15
- source_mask: int32 [256, 512], P('rows', 'cols'), may hold values 0 or 1
- profile: float32 [8, 48], replicated, may hold values from 0.1 to 1
Outputs:
- final_conc: float32 [8, 48, 256, 512], P(None, None, 'rows', 'cols')
- deposit: float32 [8, 256, 512], P(None, 'rows', 'cols')
The draws below stay inside these ranges and needn't reach their ends.
All inputs are finite; a program needn't handle non-finite values. No bound on the sum of `source_mask` on one device may be relied on, other than what follows from the above.
Results may differ from the reference program's by a relative error of at most 0.0013.
Values may be sent and summed in bfloat16 or wider, within the bound.
No kernel may reach another device: no remote copies, remote signals or barrier semaphores. Data moves between devices by JAX's collectives and lax.ppermute only.
A program may use at most 128 MiB of HBM per device.

```python
import math
import jax
import jax.numpy as jnp

BINS = 8
ZL = 48
LN = 137
RD = 8
CD = 128
NC_DEV = 2048
CAP = 64
STEPS = 3
SLOTS = 2048
NY = 256
NX = 512
NWP_COLS = 65536
N_ROWS = 32
N_COLS = 4


def draw_conc(key, part):
    shape = (BINS, ZL, NY, NX)
    pick_key = jax.random.fold_in(key, 11)
    high_key = jax.random.fold_in(key, 12)
    low_key = jax.random.fold_in(key, 13)
    heavy = jax.random.bernoulli(pick_key, 0.5, shape)
    high_part = jax.random.uniform(high_key, shape, jnp.float32)
    low_part = jax.random.uniform(low_key, shape, jnp.float32)
    values = jnp.where(heavy, 1.5 + 0.5 * high_part, 0.5 * low_part)
    return values.astype(jnp.float32)


def draw_nwp(key, part):
    shape = (2, LN, NWP_COLS)
    base = jax.random.uniform(jax.random.fold_in(key, 21), shape, jnp.float32, -1.0, 1.0)
    values = 0.29 * base
    return values.astype(jnp.bfloat16)


def place_ends(result, own_key, least, high):
    shape = result.shape
    index_at = [jax.random.randint(jax.random.fold_in(own_key, axis), (), 0, shape[axis]) for axis in range(len(shape))]
    result = result.at[tuple(index_at)].set(least)
    longest = shape.index(max(shape))
    index_at[longest] = (index_at[longest] + 1) % shape[longest]
    return result.at[tuple(index_at)].set(high)


def shard_levels(key, dims, shards, least, largest):
    def one(dim, blocks):
        steps = jax.random.uniform(jax.random.fold_in(jax.random.fold_in(key, 6), dim), (blocks,), jnp.float32, least / len(shards), largest / len(shards))
        return jnp.repeat(jnp.exp(steps), dims[dim] // blocks).reshape((-1,) + (1,) * (len(dims) - dim - 1))

    factor_of = one(*shards[0])
    for cut in shards[1:]:
        factor_of = factor_of * one(*cut)
    return factor_of


def setup_inputs(seed: int = 0) -> dict:
    arg_keys = jax.random.split(jax.random.key(seed), 11)
    conc = draw_conc(jax.random.fold_in(arg_keys[10], 71), 0)
    nwp = draw_nwp(jax.random.fold_in(arg_keys[10], 71), 0)
    lev_lo = place_ends(jax.random.randint(arg_keys[2], (ZL,), 0, LN - 1), jax.random.fold_in(arg_keys[2], 1), 0, (LN - 1) - 1).astype(jnp.int32)
    frac = jnp.clip(jax.random.uniform(arg_keys[3], (ZL,), jnp.float32, 0.0, 1.0), 0.0, 1.0)
    pick = place_ends(jax.random.randint(arg_keys[4], (N_ROWS, N_COLS, N_ROWS, CAP), 0, NC_DEV), jax.random.fold_in(arg_keys[4], 1), 0, NC_DEV - 1).astype(jnp.int32)
    corner_slot = place_ends(jax.random.randint(arg_keys[5], (4, NY, NX), 0, SLOTS), jax.random.fold_in(arg_keys[5], 1), 0, SLOTS - 1).astype(jnp.int32)
    corner_wt = jnp.clip(jnp.exp(math.log(1.0) - 1.3862944 * jax.random.uniform(arg_keys[6], (4, NY, NX), jnp.float32) ** shard_levels(arg_keys[6], (4, NY, NX), ((1, 32), (2, 4)), -0.2, 0.2)), 0.25, 1.0)
    settle = jnp.clip(jnp.exp(jax.random.uniform(arg_keys[7], (BINS,), jnp.float32, math.log(0.015), math.log(0.15))), 0.015, 0.15)
    source_mask = place_ends((jax.random.randint(arg_keys[8], (NY, NX), 0, 16) < 1).astype(jnp.int32), jax.random.fold_in(arg_keys[8], 1), 0, 1)
    profile = jnp.clip(jnp.exp(jax.random.uniform(arg_keys[9], (BINS, ZL), jnp.float32, math.log(0.1), math.log(1.0))), 0.1, 1.0)
    return dict(conc=conc, nwp=nwp, lev_lo=lev_lo, frac=frac, pick=pick, corner_slot=corner_slot, corner_wt=corner_wt, settle=settle, source_mask=source_mask, profile=profile)


KAPPA = 0.05


def vertical(columns, lev_lo, frac):
    lower = jnp.take(columns, lev_lo, axis=1).astype(jnp.float32)
    upper = jnp.take(columns, lev_lo + 1, axis=1).astype(jnp.float32)
    share = frac[None, :, None]
    return ((1.0 - share) * lower + share * upper).astype(jnp.bfloat16)


def horizontal(levels, slots, corner_wt):
    weight_sum = jnp.sum(corner_wt, axis=0)
    norm_wt = corner_wt / weight_sum
    winds = None
    for corner in range(4):
        values = jnp.take(levels, slots[corner], axis=2).astype(jnp.float32)
        term = norm_wt[corner] * values
        winds = term if winds is None else winds + term
    return winds


def advance(padded, winds, emission, settle):
    east = 0.5 * (winds[0][:, :, 1:] + winds[0][:, :, :-1])
    north = 0.5 * (winds[1][:, 1:, :] + winds[1][:, :-1, :])
    flux_x = jnp.maximum(east, 0.0) * padded[..., :, :-1] + jnp.minimum(east, 0.0) * padded[..., :, 1:]
    flux_y = jnp.maximum(north, 0.0) * padded[..., :-1, :] + jnp.minimum(north, 0.0) * padded[..., 1:, :]
    div_x = (flux_x[..., 1:] - flux_x[..., :-1])[..., 1:-1, :]
    div_y = (flux_y[..., 1:, :] - flux_y[..., :-1, :])[..., :, 1:-1]
    centre = padded[..., 1:-1, 1:-1]
    lap = padded[..., 2:, 1:-1] + padded[..., :-2, 1:-1] + padded[..., 1:-1, 2:] + padded[..., 1:-1, :-2] - 4.0 * centre
    falling = settle[:, None, None, None] * centre
    arriving = jnp.concatenate([jnp.zeros_like(falling[:, :1]), falling[:, :-1]], axis=1)
    fresh = centre - div_x - div_y + KAPPA * lap - falling + arriving + emission
    return fresh, falling[:, -1]


def reference(conc, nwp, lev_lo, frac, pick, corner_slot, corner_wt, settle, source_mask, profile):
    levels = vertical(nwp, lev_lo, frac)
    based = pick + (jnp.arange(N_ROWS, dtype=jnp.int32) * NC_DEV)[:, None, None, None]
    table = jnp.transpose(based, (2, 1, 0, 3)).reshape(N_ROWS, N_COLS, SLOTS)
    row_of = jnp.arange(NY, dtype=jnp.int32) // RD
    col_of = jnp.arange(NX, dtype=jnp.int32) // CD
    sources = table[row_of[None, :, None], col_of[None, None, :], corner_slot]
    winds = horizontal(levels, sources, corner_wt)
    emission = source_mask.astype(jnp.float32)[None, None] * profile[:, :, None, None]
    widths = ((0, 0), (0, 0), (1, 1), (1, 1))
    wind_pad = jnp.pad(winds, widths)
    state = conc
    deposit = jnp.zeros((BINS, NY, NX), jnp.float32)
    for step in range(STEPS):
        state, fallen = advance(jnp.pad(state, widths), wind_pad, emission, settle)
        deposit = deposit + fallen
    return state, deposit
```

```python
import functools

import jax
import jax.numpy as jnp
from jax import lax
from jax.experimental import pallas as pl
from jax.experimental.pallas import tpu as pltpu
from jax.sharding import PartitionSpec as P

STEPS = 3
KAPPA = 0.05
HALO = STEPS
LANES = 128
STRIP = 10
STRIP_ROWS = 12
F32 = jnp.float32
BF16 = jnp.bfloat16
VMEM_LIMIT = 48 * 1024 * 1024


def lane_ids(shape):
    return lax.broadcasted_iota(jnp.int32, shape, len(shape) - 1)


def roll_lanes(x, shift):
    return pltpu.roll(x, shift % LANES, x.ndim - 1)


def call(kernel, out_shape, args, scratch=(), flops=0, smem=()):
    moved = sum(a.size * a.dtype.itemsize for a in args) + sum(
        s.size * s.dtype.itemsize for s in jax.tree.leaves(out_shape)
    )
    return pl.pallas_call(
        kernel,
        out_shape=out_shape,
        in_specs=[
            pl.BlockSpec(memory_space=pltpu.SMEM if i in smem else pltpu.VMEM)
            for i in range(len(args))
        ],
        out_specs=jax.tree.map(lambda _: pl.BlockSpec(memory_space=pltpu.VMEM), out_shape),
        scratch_shapes=list(scratch),
        compiler_params=pltpu.CompilerParams(vmem_limit_bytes=VMEM_LIMIT),
        cost_estimate=pl.CostEstimate(flops=flops, bytes_accessed=moved, transcendentals=0),
    )(*args)


def select_kernel(lev_ref, frac_ref, pick_ref, nwp_ref, out_ref):
    fields, levels_in, count = nwp_ref.shape
    kept = lev_ref.shape[1]
    ids = lax.broadcasted_iota(jnp.int32, (levels_in, kept), 0)
    low, share = lev_ref[...], frac_ref[...]
    weight = jnp.where(ids == low, 1.0 - share, 0.0) + jnp.where(ids == low + 1, share, 0.0)
    parts = []
    for _ in range(3):
        part = weight.astype(BF16)
        weight = weight - part.astype(F32)
        parts.append(part)
    rows = []
    for field in range(fields):
        mixed = None
        for part in parts:
            term = lax.dot_general(
                part, nwp_ref[field], (((0,), (0,)), ((), ())), preferred_element_type=F32
            )
            mixed = term if mixed is None else mixed + term
        rows.append(mixed.astype(BF16))
    levels = jnp.concatenate(rows, axis=0)
    half = LANES // 2
    width = 2 * LANES
    columns = lax.broadcasted_iota(jnp.int32, (count, width), 0)
    first = lane_ids((kept, LANES)) < half
    for block in range(pick_ref.shape[1] // width):
        wanted = pick_ref[:, block * width : (block + 1) * width]
        hit = jnp.where(columns == wanted, 1.0, 0.0).astype(BF16)
        got = jnp.dot(levels, hit, preferred_element_type=F32)
        for h in range(2):
            east = got[:kept, h * LANES : (h + 1) * LANES]
            north = got[kept:, h * LANES : (h + 1) * LANES]
            out_ref[4 * block + 2 * h] = jnp.where(first, east, roll_lanes(north, half)).astype(BF16)
            out_ref[4 * block + 2 * h + 1] = jnp.where(
                first, roll_lanes(east, half), north
            ).astype(BF16)


def horizontal_kernel(recv_ref, slot_ref, wt_ref, winds_ref, a_ref, b_ref, lev_ref):
    kept = recv_ref.shape[1]
    half = LANES // 2
    first = lane_ids((kept, LANES)) < half
    for pair in range(recv_ref.shape[0] // 2):
        one = recv_ref[2 * pair].astype(F32)
        two = recv_ref[2 * pair + 1].astype(F32)
        at = slice(pair * LANES, (pair + 1) * LANES)
        lev_ref[:kept, at] = jnp.where(first, one, roll_lanes(two, half)).astype(BF16)
        lev_ref[kept:, at] = jnp.where(first, roll_lanes(one, half), two).astype(BF16)
    slots = [slot_ref[q] for q in range(4)]
    raw = [wt_ref[q] for q in range(4)]
    total = raw[0] + raw[1] + raw[2] + raw[3]
    norm = [w / total for w in raw]
    merged = []
    for q in range(4):
        share = None
        for other in range(4):
            term = jnp.where(slots[q] == slots[other], norm[other], 0.0)
            share = term if share is None else share + term
        merged.append(share)
    count = lev_ref.shape[1]
    chunk = 512
    rows = slot_ref.shape[1]
    for y in range(rows):
        acc = None
        for base in range(0, count, chunk):
            ids = lax.broadcasted_iota(jnp.int32, (chunk, LANES), 0) + base
            table = jnp.zeros((chunk, LANES), F32)
            for q in range(4):
                table = jnp.where(
                    ids == slots[q][y : y + 1], merged[q][y : y + 1], table
                )
            high = table.astype(BF16)
            low = (table - high.astype(F32)).astype(BF16)
            lev = lev_ref[:, base : base + chunk]
            term = jnp.dot(lev, high, preferred_element_type=F32) + jnp.dot(
                lev, low, preferred_element_type=F32
            )
            acc = term if acc is None else acc + term
        winds_ref[y] = acc
    odd = lax.axis_index("rows") % 2 == 1
    for j in range(HALO):
        upper = winds_ref[j]
        lower = winds_ref[rows - HALO + j]
        a_ref[j] = jnp.where(odd, upper, lower).astype(BF16)
        b_ref[j] = jnp.where(odd, lower, upper).astype(BF16)


def swap(array, axis, first):
    peers = lax.axis_size(axis)
    start = 0 if first else 1
    pairs = []
    for i in range(start, peers - 1, 2):
        pairs += [(i, i + 1), (i + 1, i)]
    return lax.ppermute(array, axis, pairs)


def strip_parts(load, shape):
    lanes = lane_ids(shape)
    own = jnp.zeros(shape, F32)
    left = jnp.zeros(shape, F32)
    right = jnp.zeros(shape, F32)
    for i in range(STRIP_ROWS):
        row = load(i - 2)
        base = STRIP * i
        at = lanes - base
        own = jnp.where((at >= 3) & (at < 5), roll_lanes(row, base + 3), own)
        own = jnp.where((at >= 5) & (at < 7), roll_lanes(row, base + 5 - 126), own)
        left = jnp.where((at >= 7) & (at < 10), roll_lanes(row, base + 7), left)
        right = jnp.where((at >= 0) & (at < 3), roll_lanes(row, base - 125), right)
    return own, left, right


def wind_strip_kernel(winds_ref, ra_ref, rb_ref, own_ref, a_ref, b_ref):
    row_odd = lax.axis_index("rows") % 2 == 1
    col_odd = lax.axis_index("cols") % 2 == 1
    rows = winds_ref.shape[0]

    def load(y):
        if 0 <= y < rows:
            return winds_ref[y].astype(BF16).astype(F32)
        j = y + HALO if y < 0 else y - rows
        got_a, got_b = ra_ref[j].astype(F32), rb_ref[j].astype(F32)
        above = jnp.where(row_odd, got_a, got_b)
        below = jnp.where(row_odd, got_b, got_a)
        return above if y < 0 else below

    own, left, right = strip_parts(load, winds_ref.shape[1:])
    own_ref[...] = own.astype(BF16)
    a_ref[...] = jnp.where(col_odd, left, right).astype(BF16)
    b_ref[...] = jnp.where(col_odd, right, left).astype(BF16)


def conc_edge_kernel(conc_ref, mask_ref, a_ref, b_ref):
    odd = lax.axis_index("rows") % 2 == 1
    bins = conc_ref.shape[0] // (mask_ref.shape[0] * (a_ref.shape[1] - 1))
    levels = a_ref.shape[1] - 1
    rows = mask_ref.shape[0]

    def level(k, carry):
        for j in range(HALO):
            upper = conc_ref[pl.ds(k * rows + j, bins, stride=levels * rows), :]
            lower = conc_ref[pl.ds(k * rows + rows - HALO + j, bins, stride=levels * rows), :]
            a_ref[j, k] = jnp.where(odd, upper, lower)
            b_ref[j, k] = jnp.where(odd, lower, upper)
        return carry

    lax.fori_loop(0, levels, level, 0, unroll=4)
    mask = mask_ref[...].astype(F32)
    for j in range(HALO):
        upper = jnp.broadcast_to(mask[j : j + 1], (bins, LANES))
        lower = jnp.broadcast_to(mask[rows - HALO + j : rows - HALO + j + 1], (bins, LANES))
        a_ref[j, levels] = jnp.where(odd, upper, lower)
        b_ref[j, levels] = jnp.where(odd, lower, upper)


def conc_strip_kernel(conc_ref, mask_ref, ra_ref, rb_ref, own_ref, a_ref, b_ref):
    row_odd = lax.axis_index("rows") % 2 == 1
    col_odd = lax.axis_index("cols") % 2 == 1
    levels = ra_ref.shape[1] - 1
    bins = ra_ref.shape[2]
    rows = mask_ref.shape[0]

    def halo(y, k):
        j = y + HALO if y < 0 else y - rows
        got_a, got_b = ra_ref[j, k], rb_ref[j, k]
        return jnp.where(row_odd == (y < 0), got_a, got_b)

    def store(k, load):
        own, left, right = strip_parts(load, (bins, LANES))
        own_ref[k] = own
        a_ref[k] = jnp.where(col_odd, left, right)
        b_ref[k] = jnp.where(col_odd, right, left)

    def level(k, carry):
        def load(y):
            if 0 <= y < rows:
                return conc_ref[pl.ds(k * rows + y, bins, stride=levels * rows), :]
            return halo(y, k)

        store(k, load)
        return carry

    lax.fori_loop(0, levels, level, 0)
    mask = mask_ref[...].astype(F32)

    def load_mask(y):
        if 0 <= y < rows:
            return jnp.broadcast_to(mask[y : y + 1], (bins, LANES))
        return halo(y, levels)

    store(levels, load_mask)


def coefficients(east_w, east, east_e, north_s, north, north_n, valid):
    face_w = 0.5 * (east_w + east)
    face_e = 0.5 * (east + east_e)
    face_s = 0.5 * (north_s + north)
    face_n = 0.5 * (north + north_n)
    out_e = jnp.maximum(face_e, 0.0)
    out_n = jnp.maximum(face_n, 0.0)
    out_w = jnp.minimum(face_w, 0.0)
    out_s = jnp.minimum(face_s, 0.0)
    centre = (1.0 - 4.0 * KAPPA) - (out_e - out_w) - (out_n - out_s)
    west = KAPPA + jnp.maximum(face_w, 0.0)
    east_c = KAPPA - jnp.minimum(face_e, 0.0)
    south = KAPPA + jnp.maximum(face_s, 0.0)
    north_c = KAPPA - jnp.minimum(face_n, 0.0)
    result = (centre, west, east_c, south, north_c)
    return result if valid is None else tuple(jnp.where(valid, c, 0.0) for c in result)


def transport_kernel(
    conc_ref, mask_ref, settle_ref, profile_ref,
    ra_ref, rb_ref, own_ref, ca_ref, cb_ref,
    winds_ref, wra_ref, wrb_ref, wown_ref, wca_ref, wcb_ref,
    out_ref, deposit_ref,
    coef_ref, strip_coef_ref, prof_ref, mask_all_ref, mask_strip_ref, fall_ref, state_ref,
):
    row, col = lax.axis_index("rows"), lax.axis_index("cols")
    last_row, last_col = lax.axis_size("rows") - 1, lax.axis_size("cols") - 1
    row_odd = row % 2 == 1
    levels = ra_ref.shape[1] - 1
    bins = ra_ref.shape[2]
    rows = mask_ref.shape[0]
    tile = (bins, LANES)
    stride = levels * rows

    def halo_of(y, get_a, get_b):
        return jnp.where(row_odd == (y < 0), get_a, get_b)

    def halo_at(y):
        return y + HALO if y < 0 else y - rows

    def wind_row(y):
        if 0 <= y < rows:
            return winds_ref[y]
        j = halo_at(y)
        return halo_of(y, wra_ref[j].astype(F32), wrb_ref[j].astype(F32))

    strip = wown_ref[...].astype(F32) + wca_ref[...].astype(F32) + wcb_ref[...].astype(F32)
    strip_u, strip_v = strip[:levels], strip[levels:]
    lanes = lane_ids((levels, LANES))
    at = lanes % STRIP
    inside = (
        ((at >= 3) | (col > 0))
        & ((at < 7) | (col < last_col))
        & ((lanes >= 2 * STRIP) | (row > 0))
        & ((lanes < (2 + rows) * STRIP) | (row < last_row))
    )
    found = coefficients(
        roll_lanes(strip_u, 1), strip_u, roll_lanes(strip_u, -1),
        roll_lanes(strip_v, STRIP), strip_v, roll_lanes(strip_v, -STRIP),
        inside,
    )
    for i in range(5):
        strip_coef_ref[i] = found[i]
    for y in range(-2, rows + 2):
        u = wind_row(y)[:levels]
        base = STRIP * (y + 2)
        u_w = jnp.where(lanes == 0, roll_lanes(strip_u, -(base + 2)), roll_lanes(u, 1))
        u_e = jnp.where(
            lanes == LANES - 1, roll_lanes(strip_u, LANES - 1 - (base + 7)), roll_lanes(u, -1)
        )
        valid = None
        if y < 0:
            valid = row > 0
        elif y >= rows:
            valid = row < last_row
        found = coefficients(
            u_w, u, u_e,
            wind_row(y - 1)[levels:], wind_row(y)[levels:], wind_row(y + 1)[levels:],
            valid,
        )
        for i in range(5):
            coef_ref[5 * (y + 2) + i] = found[i]

    mask = mask_ref[...].astype(F32)
    for y in range(-2, rows + 2):
        if 0 <= y < rows:
            mask_all_ref[y + 2] = jnp.broadcast_to(mask[y : y + 1], tile)
        else:
            j = halo_at(y)
            mask_all_ref[y + 2] = halo_of(y, ra_ref[j, levels], rb_ref[j, levels])
    mask_strip_ref[...] = own_ref[levels] + ca_ref[levels] + cb_ref[levels]
    sublanes = lax.broadcasted_iota(jnp.int32, tile, 0)
    settle = jnp.zeros(tile, F32)
    for b in range(bins):
        settle = jnp.where(sublanes == b, settle_ref[b], settle)
    for k in range(levels):
        prof_ref[k] = jnp.broadcast_to(profile_ref[:, k : k + 1], tile)
    fall_ref[...] = jnp.zeros(fall_ref.shape, F32)

    tile_lanes = lane_ids(tile)
    at_west = tile_lanes == 0
    at_east = tile_lanes == LANES - 1

    def level(k, carry):
        prof = prof_ref[k]

        def spread(ref, i):
            return ref[i, pl.ds(k, bins, stride=0), :]

        state = {}
        for y in range(-HALO, rows + HALO):
            if 0 <= y < rows:
                state[y] = conc_ref[pl.ds(k * rows + y, bins, stride=stride), :]
            else:
                j = halo_at(y)
                state[y] = halo_of(y, ra_ref[j, k], rb_ref[j, k])
        edge = own_ref[k] + ca_ref[k] + cb_ref[k]
        slot = 0
        for step in range(STEPS):
            reach = STEPS - 1 - step
            fresh = {}
            for y in range(-reach, rows + reach):
                a = state[y]
                base = STRIP * (y + 2)
                a_w = jnp.where(at_west, roll_lanes(edge, -(base + 2)), roll_lanes(a, 1))
                a_e = jnp.where(
                    at_east, roll_lanes(edge, LANES - 1 - (base + 7)), roll_lanes(a, -1)
                )
                c = [spread(coef_ref, 5 * (y + 2) + i) for i in range(5)]
                fall = settle * a
                source = fall_ref[slot] + prof * mask_all_ref[y + 2]
                fall_ref[slot] = fall
                fresh[y] = (
                    (c[0] * a - fall)
                    + (c[1] * a_w + c[2] * a_e)
                    + (c[3] * state[y - 1] + c[4] * state[y + 1])
                    + source
                )
                slot += 1
            if reach:
                c = [spread(strip_coef_ref, i) for i in range(5)]
                fall = settle * edge
                source = fall_ref[slot] + prof * mask_strip_ref[...]
                fall_ref[slot] = fall
                edge = (
                    (c[0] * edge - fall)
                    + (c[1] * roll_lanes(edge, 1) + c[2] * roll_lanes(edge, -1))
                    + (c[3] * roll_lanes(edge, STRIP) + c[4] * roll_lanes(edge, -STRIP))
                    + source
                )
                slot += 1
            state = fresh
        for y in range(rows):
            out_ref[pl.ds(k * rows + y, bins, stride=stride), :] = state[y]
        return carry

    lax.fori_loop(0, levels, level, 0)
    first, second, third = 2, rows + 2 * 2 + 1 + 1, (rows + 2 * 2 + 1) + (rows + 2 + 1)
    for y in range(rows):
        deposit_ref[pl.ds(y, bins, stride=rows), :] = (
            fall_ref[first + y] + fall_ref[second + y] + fall_ref[third + y]
        )


def per_device(conc, nwp, lev_lo, frac, pick, corner_slot, corner_wt, settle, source_mask, profile):
    bins, levels, rows, cols = conc.shape
    peers = pick.shape[2]
    shape = jax.ShapeDtypeStruct
    flat = conc.reshape(bins * levels * rows, cols)

    sent = call(
        select_kernel,
        shape((peers, levels, LANES), BF16),
        (lev_lo.reshape(1, -1), frac.reshape(1, -1), pick.reshape(1, -1), nwp),
        flops=2 * 2 * levels * 2048 * 2048,
    )
    received = lax.all_to_all(sent, "rows", split_axis=0, concat_axis=0, tiled=True)

    edge_rows = shape((HALO, levels + 1, bins, cols), F32)
    strips = shape((levels + 1, bins, LANES), F32)
    ca, cb = call(conc_edge_kernel, (edge_rows, edge_rows), (flat, source_mask))
    ra, rb = swap(ca, "rows", True), swap(cb, "rows", False)
    own, sa, sb = call(conc_strip_kernel, (strips, strips, strips), (flat, source_mask, ra, rb))
    xa, xb = swap(sa, "cols", True), swap(sb, "cols", False)

    wind_rows = shape((HALO, 2 * levels, cols), BF16)
    winds, wa, wb = call(
        horizontal_kernel,
        (shape((rows, 2 * levels, cols), F32), wind_rows, wind_rows),
        (received, corner_slot, corner_wt),
        scratch=(pltpu.VMEM((2 * levels, peers * LANES // 2), BF16),),
        flops=2 * 2 * 2 * levels * 2048 * 1024,
    )
    wra, wrb = swap(wa, "rows", True), swap(wb, "rows", False)
    wind_strip = shape((2 * levels, LANES), BF16)
    wown, wsa, wsb = call(
        wind_strip_kernel, (wind_strip, wind_strip, wind_strip), (winds, wra, wrb)
    )
    wxa, wxb = swap(wsa, "cols", True), swap(wsb, "cols", False)

    tile = (bins, LANES)
    updates = sum(rows + 2 * (STEPS - 1 - s) for s in range(STEPS)) + STEPS - 1
    final, deposit = call(
        transport_kernel,
        (shape(flat.shape, F32), shape((bins * rows, cols), F32)),
        (flat, source_mask, settle, profile, ra, rb, own, xa, xb,
         winds, wra, wrb, wown, wxa, wxb),
        scratch=(
            pltpu.VMEM((5 * (rows + 4), levels, LANES), F32),
            pltpu.VMEM((5, levels, LANES), F32),
            pltpu.VMEM((levels,) + tile, F32),
            pltpu.VMEM((rows + 4,) + tile, F32),
            pltpu.VMEM(tile, F32),
            pltpu.VMEM((updates,) + tile, F32),
            pltpu.VMEM(tile, F32),
        ),
        smem=(2,),
        flops=16 * updates * levels * bins * LANES,
    )
    return final.reshape(conc.shape), deposit.reshape(bins, rows, cols)


def solution(mesh):
    placed = (
        P(None, None, "rows", "cols"),
        P(None, None, "rows"),
        P(),
        P(),
        P("rows", "cols", None, None),
        P(None, "rows", "cols"),
        P(None, "rows", "cols"),
        P(),
        P("rows", "cols"),
        P(),
    )
    return jax.shard_map(
        per_device,
        mesh=mesh,
        in_specs=placed,
        out_specs=(P(None, None, "rows", "cols"), P(None, "rows", "cols")),
        check_vma=False,
    )
```

```python
import functools

import jax
import jax.numpy as jnp
from jax import lax
from jax.experimental import pallas as pl
from jax.experimental.pallas import tpu as pltpu
from jax.sharding import PartitionSpec as P

STEPS = 3
KAPPA = 0.05
HALO = STEPS
LANES = 128
STRIP = 10
STRIP_ROWS = 12
F32 = jnp.float32
BF16 = jnp.bfloat16
VMEM_LIMIT = 48 * 1024 * 1024


def lane_ids(shape):
    return lax.broadcasted_iota(jnp.int32, shape, len(shape) - 1)


def roll_lanes(x, shift):
    return pltpu.roll(x, shift % LANES, x.ndim - 1)


def call(kernel, out_shape, args, scratch=(), flops=0, smem=()):
    moved = sum(a.size * a.dtype.itemsize for a in args) + sum(
        s.size * s.dtype.itemsize for s in jax.tree.leaves(out_shape)
    )
    return pl.pallas_call(
        kernel,
        out_shape=out_shape,
        in_specs=[
            pl.BlockSpec(memory_space=pltpu.SMEM if i in smem else pltpu.VMEM)
            for i in range(len(args))
        ],
        out_specs=jax.tree.map(lambda _: pl.BlockSpec(memory_space=pltpu.VMEM), out_shape),
        scratch_shapes=list(scratch),
        compiler_params=pltpu.CompilerParams(vmem_limit_bytes=VMEM_LIMIT),
        cost_estimate=pl.CostEstimate(flops=flops, bytes_accessed=moved, transcendentals=0),
    )(*args)


def select_kernel(lev_ref, frac_ref, pick_ref, nwp_ref, out_ref):
    fields, levels_in, count = nwp_ref.shape
    kept = lev_ref.shape[1]
    ids = lax.broadcasted_iota(jnp.int32, (levels_in, kept), 0)
    low, share = lev_ref[...], frac_ref[...]
    weight = jnp.where(ids == low, 1.0 - share, 0.0) + jnp.where(ids == low + 1, share, 0.0)
    parts = []
    for _ in range(3):
        part = weight.astype(BF16)
        weight = weight - part.astype(F32)
        parts.append(part)
    rows = []
    for field in range(fields):
        mixed = None
        for part in parts:
            term = lax.dot_general(
                part, nwp_ref[field], (((0,), (0,)), ((), ())), preferred_element_type=F32
            )
            mixed = term if mixed is None else mixed + term
        rows.append(mixed.astype(BF16))
    levels = jnp.concatenate(rows, axis=0)
    half = LANES // 2
    width = 2 * LANES
    columns = lax.broadcasted_iota(jnp.int32, (count, width), 0)
    first = lane_ids((kept, LANES)) < half
    for block in range(pick_ref.shape[1] // width):
        wanted = pick_ref[:, block * width : (block + 1) * width]
        hit = jnp.where(columns == wanted, 1.0, 0.0).astype(BF16)
        got = jnp.dot(levels, hit, preferred_element_type=F32)
        for h in range(2):
            east = got[:kept, h * LANES : (h + 1) * LANES]
            north = got[kept:, h * LANES : (h + 1) * LANES]
            out_ref[4 * block + 2 * h] = jnp.where(first, east, roll_lanes(north, half)).astype(BF16)
            out_ref[4 * block + 2 * h + 1] = jnp.where(
                first, roll_lanes(east, half), north
            ).astype(BF16)


def horizontal_kernel(recv_ref, slot_ref, wt_ref, winds_ref, a_ref, b_ref, lev_ref):
    kept = recv_ref.shape[1]
    half = LANES // 2
    first = lane_ids((kept, LANES)) < half
    for pair in range(recv_ref.shape[0] // 2):
        one = recv_ref[2 * pair].astype(F32)
        two = recv_ref[2 * pair + 1].astype(F32)
        at = slice(pair * LANES, (pair + 1) * LANES)
        lev_ref[:kept, at] = jnp.where(first, one, roll_lanes(two, half)).astype(BF16)
        lev_ref[kept:, at] = jnp.where(first, roll_lanes(one, half), two).astype(BF16)
    slots = [slot_ref[q] for q in range(4)]
    raw = [wt_ref[q] for q in range(4)]
    total = raw[0] + raw[1] + raw[2] + raw[3]
    norm = [w / total for w in raw]
    merged = []
    for q in range(4):
        share = None
        for other in range(4):
            term = jnp.where(slots[q] == slots[other], norm[other], 0.0)
            share = term if share is None else share + term
        merged.append(share)
    count = lev_ref.shape[1]
    chunk = 512
    rows = slot_ref.shape[1]
    for y in range(rows):
        acc = None
        for base in range(0, count, chunk):
            ids = lax.broadcasted_iota(jnp.int32, (chunk, LANES), 0) + base
            table = jnp.zeros((chunk, LANES), F32)
            for q in range(4):
                table = jnp.where(
                    ids == slots[q][y : y + 1], merged[q][y : y + 1], table
                )
            high = table.astype(BF16)
            low = (table - high.astype(F32)).astype(BF16)
            lev = lev_ref[:, base : base + chunk]
            term = jnp.dot(lev, high, preferred_element_type=F32) + jnp.dot(
                lev, low, preferred_element_type=F32
            )
            acc = term if acc is None else acc + term
        winds_ref[y] = acc
    odd = lax.axis_index("rows") % 2 == 1
    for j in range(HALO):
        upper = winds_ref[j]
        lower = winds_ref[rows - HALO + j]
        a_ref[j] = jnp.where(odd, upper, lower).astype(BF16)
        b_ref[j] = jnp.where(odd, lower, upper).astype(BF16)


def swap(array, axis, first):
    peers = lax.axis_size(axis)
    start = 0 if first else 1
    pairs = []
    for i in range(start, peers - 1, 2):
        pairs += [(i, i + 1), (i + 1, i)]
    return lax.ppermute(array, axis, pairs)


def strip_select():
    lane = lane_ids((LANES, LANES))
    column = lax.broadcasted_iota(jnp.int32, (LANES, LANES), 0)
    chosen = []
    for i in range(STRIP_ROWS):
        at = lane - STRIP * i
        source = jnp.where(at < 3, at + 125, jnp.where(at < 5, at - 3, jnp.where(at < 7, at + 121, at - 7)))
        hit = (source == column) & (at >= 0) & (at < STRIP)
        chosen.append(jnp.where(hit, 1.0, 0.0).astype(BF16))
    return chosen


def whole_strip(mine, got_a, got_b, at, odd):
    from_left = jnp.where(odd, got_a, got_b)
    from_right = jnp.where(odd, got_b, got_a)
    return jnp.where(at < 3, from_left, jnp.where(at < 7, mine, from_right))


def wind_strip_kernel(winds_ref, ra_ref, rb_ref, strip_ref):
    row_odd = lax.axis_index("rows") % 2 == 1
    rows = winds_ref.shape[0]
    chosen = strip_select()
    total = None
    for i in range(STRIP_ROWS):
        y = i - 2
        if 0 <= y < rows:
            line = winds_ref[y].astype(BF16)
        else:
            j = y + HALO if y < 0 else y - rows
            line = jnp.where(row_odd == (y < 0), ra_ref[j], rb_ref[j])
        term = jnp.dot(line, chosen[i], preferred_element_type=F32)
        total = term if total is None else total + term
    strip_ref[...] = total.astype(BF16)


def conc_edge_kernel(conc_ref, mask_ref, a_ref, b_ref):
    odd = lax.axis_index("rows") % 2 == 1
    bins = conc_ref.shape[0] // (mask_ref.shape[0] * (a_ref.shape[1] - 1))
    levels = a_ref.shape[1] - 1
    rows = mask_ref.shape[0]

    def level(k, carry):
        for j in range(HALO):
            upper = conc_ref[pl.ds(k * rows + j, bins, stride=levels * rows), :]
            lower = conc_ref[pl.ds(k * rows + rows - HALO + j, bins, stride=levels * rows), :]
            a_ref[j, k] = jnp.where(odd, upper, lower)
            b_ref[j, k] = jnp.where(odd, lower, upper)
        return carry

    lax.fori_loop(0, levels, level, 0, unroll=4)
    mask = mask_ref[...].astype(F32)
    for j in range(HALO):
        upper = jnp.broadcast_to(mask[j : j + 1], (bins, LANES))
        lower = jnp.broadcast_to(mask[rows - HALO + j : rows - HALO + j + 1], (bins, LANES))
        a_ref[j, levels] = jnp.where(odd, upper, lower)
        b_ref[j, levels] = jnp.where(odd, lower, upper)


def conc_strip_kernel(conc_ref, mask_ref, ra_ref, rb_ref, strip_ref, high_ref, low_ref):
    row_odd = lax.axis_index("rows") % 2 == 1
    levels = ra_ref.shape[1] - 1
    bins = ra_ref.shape[2]
    rows = mask_ref.shape[0]
    mask = mask_ref[...].astype(F32)
    chosen = strip_select()
    total = None
    for i in range(STRIP_ROWS):
        y = i - 2
        for k in range(0, levels + 1, 2):
            pair = []
            for level in (k, min(k + 1, levels)):
                if not 0 <= y < rows:
                    j = y + HALO if y < 0 else y - rows
                    pair.append(jnp.where(row_odd == (y < 0), ra_ref[j, level], rb_ref[j, level]))
                elif level < levels:
                    pair.append(conc_ref[pl.ds(level * rows + y, bins, stride=levels * rows), :])
                else:
                    pair.append(jnp.broadcast_to(mask[y : y + 1], (bins, LANES)))
            both = jnp.concatenate(pair, axis=0)
            high = both.astype(BF16)
            at = slice(k * bins, (k + 2) * bins)
            high_ref[i % 2, at] = high
            low_ref[i % 2, at] = (both - high.astype(F32)).astype(BF16)
        term = jnp.dot(high_ref[i % 2], chosen[i], preferred_element_type=F32) + jnp.dot(
            low_ref[i % 2], chosen[i], preferred_element_type=F32
        )
        total = term if total is None else total + term
    strip_ref[...] = total[: (levels + 1) * bins]


def coefficients(east_w, east, east_e, north_s, north, north_n, valid):
    face_w = 0.5 * (east_w + east)
    face_e = 0.5 * (east + east_e)
    face_s = 0.5 * (north_s + north)
    face_n = 0.5 * (north + north_n)
    out_e = jnp.maximum(face_e, 0.0)
    out_n = jnp.maximum(face_n, 0.0)
    out_w = jnp.minimum(face_w, 0.0)
    out_s = jnp.minimum(face_s, 0.0)
    centre = (1.0 - 4.0 * KAPPA) - (out_e - out_w) - (out_n - out_s)
    west = KAPPA + jnp.maximum(face_w, 0.0)
    east_c = KAPPA - jnp.minimum(face_e, 0.0)
    south = KAPPA + jnp.maximum(face_s, 0.0)
    north_c = KAPPA - jnp.minimum(face_n, 0.0)
    result = (centre, west, east_c, south, north_c)
    return result if valid is None else tuple(jnp.where(valid, c, 0.0) for c in result)


def transport_kernel(
    conc_ref, mask_ref, settle_ref, profile_ref,
    ra_ref, rb_ref, own_ref, ca_ref, cb_ref,
    winds_ref, wra_ref, wrb_ref, wown_ref, wca_ref, wcb_ref,
    out_ref, deposit_ref,
    coef_ref, strip_coef_ref, edge_ref, bound_ref, source_ref, fall_ref,
):
    row, col = lax.axis_index("rows"), lax.axis_index("cols")
    last_row, last_col = lax.axis_size("rows") - 1, lax.axis_size("cols") - 1
    row_odd, col_odd = row % 2 == 1, col % 2 == 1
    levels = ra_ref.shape[1] - 1
    bins = ra_ref.shape[2]
    rows = mask_ref.shape[0]
    tile = (bins, LANES)
    stride = levels * rows

    def halo_of(y, get_a, get_b):
        return jnp.where(row_odd == (y < 0), get_a, get_b)

    def halo_at(y):
        return y + HALO if y < 0 else y - rows

    def wind_row(y):
        if 0 <= y < rows:
            return winds_ref[y]
        j = halo_at(y)
        return halo_of(y, wra_ref[j].astype(F32), wrb_ref[j].astype(F32))

    lanes = lane_ids((levels, LANES))
    at = lanes % STRIP
    wide = lane_ids((2 * levels, LANES)) % STRIP
    strip = whole_strip(
        wown_ref[...].astype(F32), wca_ref[...].astype(F32), wcb_ref[...].astype(F32), wide, col_odd
    )
    strip_u, strip_v = strip[:levels], strip[levels:]
    inside = (
        ((at >= 3) | (col > 0))
        & ((at < 7) | (col < last_col))
        & ((lanes >= 2 * STRIP) | (row > 0))
        & ((lanes < (2 + rows) * STRIP) | (row < last_row))
    )
    found = coefficients(
        roll_lanes(strip_u, 1), strip_u, roll_lanes(strip_u, -1),
        roll_lanes(strip_v, STRIP), strip_v, roll_lanes(strip_v, -STRIP),
        inside,
    )
    for i in range(5):
        strip_coef_ref[i] = found[i]
    for y in range(-2, rows + 2):
        u = wind_row(y)[:levels]
        base = STRIP * (y + 2)
        u_w = jnp.where(lanes == 0, roll_lanes(strip_u, -(base + 2)), roll_lanes(u, 1))
        u_e = jnp.where(
            lanes == LANES - 1, roll_lanes(strip_u, LANES - 1 - (base + 7)), roll_lanes(u, -1)
        )
        valid = None
        if y < 0:
            valid = row > 0
        elif y >= rows:
            valid = row < last_row
        centre, west, east, south, north = coefficients(
            u_w, u, u_e,
            wind_row(y - 1)[levels:], wind_row(y)[levels:], wind_row(y + 1)[levels:],
            valid,
        )
        west = jnp.where(lanes == 0, 0.0, west)
        east = jnp.where(lanes == LANES - 1, 0.0, east)
        for i, c in enumerate((centre, west, east, south, north)):
            coef_ref[5 * (y + 2) + i] = c

    sublanes = lax.broadcasted_iota(jnp.int32, tile, 0)
    settle = jnp.zeros(tile, F32)
    for b in range(bins):
        settle = jnp.where(sublanes == b, settle_ref[b], settle)

    tile_lanes = lane_ids(tile)
    tile_at = tile_lanes % STRIP
    spare = STRIP * STRIP_ROWS

    def edge_of(k):
        at_k = pl.ds(k * bins, bins)
        return whole_strip(own_ref[at_k, :], ca_ref[at_k, :], cb_ref[at_k, :], tile_at, col_odd)

    mask_strip = edge_of(levels)
    zero = jnp.zeros(tile, F32)
    fall_before = [zero] * (STEPS - 1)
    for k in range(levels):
        edge = edge_of(k)
        prof = jnp.broadcast_to(profile_ref[:, k : k + 1], tile)
        parts = []
        rest = prof
        for _ in range(3):
            part = rest.astype(BF16).astype(F32)
            rest = rest - part
            parts.append(part)
        emitted = prof * mask_strip
        c = [jnp.broadcast_to(strip_coef_ref[i, k : k + 1, :], tile) for i in range(5)]
        for step in range(STEPS):
            from_w = c[1] * roll_lanes(edge, 1)
            from_e = c[2] * roll_lanes(edge, -1)
            flow = jnp.where(tile_at == 3, from_w, jnp.where(tile_at == 6, from_e, 0.0))
            for i, part in enumerate(parts):
                flow = jnp.where(tile_lanes == spare + i, part, flow)
            flow = jnp.where(tile_lanes >= spare + 3, 0.0, flow)
            bound_ref[step, k * bins : (k + 1) * bins] = flow
            if step < STEPS - 1:
                fall = settle * edge
                edge = (
                    (c[0] * edge - fall)
                    + (from_w + from_e)
                    + (c[3] * roll_lanes(edge, STRIP) + c[4] * roll_lanes(edge, -STRIP))
                    + (fall_before[step] + emitted)
                )
                fall_before[step] = fall

    lane_of = lax.broadcasted_iota(jnp.int32, (LANES, LANES), 0)
    x_of = lane_ids((LANES, LANES))
    mask = mask_ref[...].astype(F32)
    spread = []
    for y in range(-2, rows + 2):
        base = STRIP * (y + 2)
        hit = ((x_of == 0) & (lane_of == base + 3)) | ((x_of == LANES - 1) & (lane_of == base + 6))
        if 0 <= y < rows:
            line = mask[y : y + 1]
        else:
            j = halo_at(y)
            line = halo_of(y, ra_ref[j, levels], rb_ref[j, levels])[:1]
        emits = (lane_of >= spare) & (lane_of < spare + 3)
        table = jnp.where(hit, 1.0, jnp.where(emits, line, 0.0)).astype(BF16)
        spread.append(jnp.concatenate([table, table], axis=0))
    slot = 0
    slots = {}
    for step in range(STEPS):
        flow = bound_ref[step]
        high = flow.astype(BF16)
        low = (flow - high.astype(F32)).astype(BF16)
        both = jnp.concatenate([high, low], axis=1)
        reach = STEPS - 1 - step
        for y in range(-reach, rows + reach):
            slots[step, y] = slot
            source_ref[slot] = jnp.dot(both, spread[y + 2], preferred_element_type=F32)
            slot += 1

    fall_ref[...] = jnp.zeros(fall_ref.shape, F32)
    unroll = 4

    def some_levels(trip, carry):
        ks = [trip * unroll + u for u in range(unroll)]

        def start_of(y, k):
            if 0 <= y < rows:
                return conc_ref[pl.ds(k * rows + y, bins, stride=stride), :]
            j = halo_at(y)
            return halo_of(y, ra_ref[j, k], rb_ref[j, k])

        coefs = [{} for _ in ks]
        states = [[{} for _ in range(STEPS + 1)] for _ in ks]
        for u, k in enumerate(ks):
            for y in (-3, -2):
                states[u][0][y] = start_of(y, k)
        for front in range(-2, rows + 4):
            for step in range(STEPS):
                y = front - step
                reach = STEPS - 1 - step
                if not -reach <= y < rows + reach:
                    continue
                index = slots[step, y]
                fall = fall_ref[index]
                for u, k in enumerate(ks):
                    state = states[u][step]
                    if step == 0:
                        state[y + 1] = start_of(y + 1, k)
                        coefs[u][y] = [
                            coef_ref[5 * (y + 2) + i, pl.ds(k, bins, stride=0), :] for i in range(5)
                        ]
                    c = coefs[u][y]
                    a = state[y]
                    source = source_ref[index, pl.ds(k * bins, bins), :] + fall
                    fall = settle * a
                    fresh = (
                        (c[0] * a - fall)
                        + (c[1] * roll_lanes(a, 1) + c[2] * roll_lanes(a, -1))
                        + (c[3] * state[y - 1] + c[4] * state[y + 1])
                        + source
                    )
                    if step < STEPS - 1:
                        states[u][step + 1][y] = fresh
                    else:
                        out_ref[pl.ds(k * rows + y, bins, stride=stride), :] = fresh
                fall_ref[index] = fall
        return carry

    lax.fori_loop(0, levels // unroll, some_levels, 0)
    for y in range(rows):
        deposit_ref[pl.ds(y, bins, stride=rows), :] = (
            fall_ref[slots[0, y]] + fall_ref[slots[1, y]] + fall_ref[slots[2, y]]
        )


def per_device(conc, nwp, lev_lo, frac, pick, corner_slot, corner_wt, settle, source_mask, profile):
    bins, levels, rows, cols = conc.shape
    peers = pick.shape[2]
    shape = jax.ShapeDtypeStruct
    flat = conc.reshape(bins * levels * rows, cols)

    sent = call(
        select_kernel,
        shape((peers, levels, LANES), BF16),
        (lev_lo.reshape(1, -1), frac.reshape(1, -1), pick.reshape(1, -1), nwp),
        flops=2 * 2 * levels * 2048 * 2048,
    )

    flat, sent = lax.optimization_barrier((flat, sent))
    received = lax.all_to_all(sent, "rows", split_axis=0, concat_axis=0, tiled=True)

    edge_rows = shape((HALO, levels + 1, bins, cols), F32)
    strips = shape(((levels + 1) * bins, LANES), F32)
    ca, cb = call(conc_edge_kernel, (edge_rows, edge_rows), (flat, source_mask))
    ra, rb = swap(ca, "rows", True), swap(cb, "rows", False)
    padded = (levels + 2) * bins
    own = call(
        conc_strip_kernel, strips, (flat, source_mask, ra, rb),
        scratch=(pltpu.VMEM((2, padded, LANES), BF16), pltpu.VMEM((2, padded, LANES), BF16)),
    )
    xa, xb = swap(own, "cols", True), swap(own, "cols", False)

    wind_rows = shape((HALO, 2 * levels, cols), BF16)
    winds, wa, wb = call(
        horizontal_kernel,
        (shape((rows, 2 * levels, cols), F32), wind_rows, wind_rows),
        (received, corner_slot, corner_wt),
        scratch=(pltpu.VMEM((2 * levels, peers * LANES // 2), BF16),),
        flops=2 * 2 * 2 * levels * 2048 * 1024,
    )
    wra, wrb = swap(wa, "rows", True), swap(wb, "rows", False)
    wown = call(wind_strip_kernel, shape((2 * levels, LANES), BF16), (winds, wra, wrb))
    wxa, wxb = swap(wown, "cols", True), swap(wown, "cols", False)

    tile = (bins, LANES)
    updates = sum(rows + 2 * (STEPS - 1 - s) for s in range(STEPS))
    final, deposit = call(
        transport_kernel,
        (shape(flat.shape, F32), shape((bins * rows, cols), F32)),
        (flat, source_mask, settle, profile, ra, rb, own, xa, xb,
         winds, wra, wrb, wown, wxa, wxb),
        scratch=(
            pltpu.VMEM((5 * (rows + 4), levels, LANES), F32),
            pltpu.VMEM((5, levels, LANES), F32),
            pltpu.VMEM(tile, F32),
            pltpu.VMEM((STEPS, levels * bins, LANES), F32),
            pltpu.VMEM((updates, levels * bins, LANES), F32),
            pltpu.VMEM((updates,) + tile, F32),
        ),
        smem=(2,),
        flops=16 * updates * levels * bins * LANES,
    )
    return final.reshape(conc.shape), deposit.reshape(bins, rows, cols)


def solution(mesh):
    placed = (
        P(None, None, "rows", "cols"),
        P(None, None, "rows"),
        P(),
        P(),
        P("rows", "cols", None, None),
        P(None, "rows", "cols"),
        P(None, "rows", "cols"),
        P(),
        P("rows", "cols"),
        P(),
    )
    return jax.shard_map(
        per_device,
        mesh=mesh,
        in_specs=placed,
        out_specs=(P(None, None, "rows", "cols"), P(None, "rows", "cols")),
        check_vma=False,
    )
```

```python
import functools

import jax
import jax.numpy as jnp
from jax import lax
from jax.experimental import pallas as pl
from jax.experimental.pallas import tpu as pltpu
from jax.sharding import PartitionSpec as P

STEPS = 3
KAPPA = 0.05
HALO = STEPS
LANES = 128
STRIP = 10
STRIP_ROWS = 12
F32 = jnp.float32
BF16 = jnp.bfloat16
SPLIT = 64
MIB = 1024 * 1024
HIDES = 50_000_000_000


def lane_ids(shape):
    return lax.broadcasted_iota(jnp.int32, shape, len(shape) - 1)


def roll_lanes(x, shift):
    return pltpu.roll(x, shift % LANES, x.ndim - 1)


def call(kernel, out_shape, args, scratch=(), flops=0, smem=(), limit=16, moved=None, out_space=pltpu.VMEM):
    if moved is None:
        moved = sum(a.size * a.dtype.itemsize for a in args) + sum(
            s.size * s.dtype.itemsize for s in jax.tree.leaves(out_shape)
        )
    return pl.pallas_call(
        kernel,
        out_shape=out_shape,
        in_specs=[
            pl.BlockSpec(memory_space=pltpu.SMEM if i in smem else pltpu.VMEM)
            for i in range(len(args))
        ],
        out_specs=jax.tree.map(lambda _: pl.BlockSpec(memory_space=out_space), out_shape),
        scratch_shapes=list(scratch),
        compiler_params=pltpu.CompilerParams(vmem_limit_bytes=limit * MIB),
        cost_estimate=pl.CostEstimate(flops=flops, bytes_accessed=moved, transcendentals=0),
    )(*args)


def select_kernel(lev_ref, frac_ref, pick_ref, nwp_ref, sent_ref, out_ref, sem):
    fields, levels_in, count = nwp_ref.shape
    kept = lev_ref.shape[1]
    ids = lax.broadcasted_iota(jnp.int32, (levels_in, kept), 0)
    low, share = lev_ref[...], frac_ref[...]
    weight = jnp.where(ids == low, 1.0 - share, 0.0) + jnp.where(ids == low + 1, share, 0.0)
    parts = []
    for _ in range(3):
        part = weight.astype(BF16)
        weight = weight - part.astype(F32)
        parts.append(part)
    rows = []
    for field in range(fields):
        mixed = None
        for part in parts:
            term = lax.dot_general(
                part, nwp_ref[field], (((0,), (0,)), ((), ())), preferred_element_type=F32
            )
            mixed = term if mixed is None else mixed + term
        rows.append(mixed.astype(BF16))
    levels = jnp.concatenate(rows, axis=0)
    half = LANES // 2
    width = 2 * LANES
    inner = lax.broadcasted_iota(jnp.int32, (SPLIT, width), 0)
    none = jnp.zeros((SPLIT, width), BF16)
    first = lane_ids((kept, LANES)) < half
    copies = []
    for block in range(pick_ref.shape[0] // 4):
        wanted = jnp.concatenate([pick_ref[4 * block + i : 4 * block + i + 1] for i in range(4)], axis=1)
        group = wanted // SPLIT
        unit = jnp.where(inner == wanted - group * SPLIT, 1.0, 0.0).astype(BF16)
        group = jnp.broadcast_to(group.astype(F32), (SPLIT, width)).astype(BF16)
        hit = jnp.concatenate([jnp.where(group == g, unit, none) for g in range(count // SPLIT)], axis=0)
        got = jnp.dot(levels, hit, preferred_element_type=F32)
        for h in range(2):
            east = got[:kept, h * LANES : (h + 1) * LANES]
            north = got[kept:, h * LANES : (h + 1) * LANES]
            out_ref[4 * block + 2 * h] = jnp.where(first, east, roll_lanes(north, half)).astype(BF16)
            out_ref[4 * block + 2 * h + 1] = jnp.where(
                first, roll_lanes(east, half), north
            ).astype(BF16)
        at = pl.ds(4 * block, 4)
        copies.append(pltpu.make_async_copy(out_ref.at[at], sent_ref.at[at], sem.at[block]))
        copies[-1].start()
    for copy in copies:
        copy.wait()


def corner_tables(slot_ref, wt_ref, count):
    slots = [slot_ref[q] for q in range(4)]
    raw = [wt_ref[q] for q in range(4)]
    total = raw[0] + raw[1] + raw[2] + raw[3]
    norm = [w / total for w in raw]
    groups, units, highs, lows = [], [], [], []
    for q in range(4):
        share = None
        for other in range(4):
            term = jnp.where(slots[q] == slots[other], norm[other], 0.0)
            share = term if share is None else share + term
        for other in range(q):
            share = jnp.where(slots[q] == slots[other], 0.0, share)
        high = share.astype(BF16).astype(F32)
        group = slots[q] // SPLIT
        groups.append(group.astype(F32))
        units.append(slots[q] - group * SPLIT)
        highs.append(high)
        lows.append(share - high)
    inner = lax.broadcasted_iota(jnp.int32, (SPLIT, LANES), 0)
    none = jnp.zeros((SPLIT, LANES), BF16)

    def tables(y):
        line = slice(y, y + 1)
        hits = [inner == units[q][line] for q in range(4)]
        group = [jnp.broadcast_to(groups[q][line], (SPLIT, LANES)).astype(BF16) for q in range(4)]
        result = []
        for parts in (highs, lows):
            own = [jnp.where(hits[q], parts[q][line], 0.0).astype(BF16) for q in range(4)]
            blocks = []
            for g in range(count // SPLIT):
                two = [jnp.where(group[q] == g, own[q], none) for q in range(4)]
                blocks.append((two[0] + two[1]) + (two[2] + two[3]))
            result.append(jnp.concatenate(blocks, axis=0))
        return result

    return tables


def horizontal_kernel(recv_ref, slot_ref, wt_ref, winds_ref, a_ref, b_ref, lev_ref):
    kept = recv_ref.shape[1]
    half = LANES // 2
    first = lane_ids((kept, LANES)) < half
    for pair in range(recv_ref.shape[0] // 2):
        one = recv_ref[2 * pair].astype(F32)
        two = recv_ref[2 * pair + 1].astype(F32)
        at = slice(pair * LANES, (pair + 1) * LANES)
        lev_ref[:kept, at] = jnp.where(first, one, roll_lanes(two, half)).astype(BF16)
        lev_ref[kept:, at] = jnp.where(first, roll_lanes(one, half), two).astype(BF16)
    rows = winds_ref.shape[0]
    lev = lev_ref[...]
    tables = corner_tables(slot_ref, wt_ref, lev_ref.shape[1])
    for y in range(0, rows, 2):
        one, two = tables(y), tables(y + 1)
        got = sum(
            jnp.dot(lev, jnp.concatenate(pair, axis=1), preferred_element_type=F32)
            for pair in zip(one, two)
        )
        winds_ref[y] = got[:, :LANES]
        winds_ref[y + 1] = got[:, LANES:]
    odd = lax.axis_index("rows") % 2 == 1
    for j in range(HALO):
        upper = winds_ref[j]
        lower = winds_ref[rows - HALO + j]
        a_ref[j] = jnp.where(odd, upper, lower).astype(BF16)
        b_ref[j] = jnp.where(odd, lower, upper).astype(BF16)


def swap(array, axis, first):
    peers = lax.axis_size(axis)
    start = 0 if first else 1
    pairs = []
    for i in range(start, peers - 1, 2):
        pairs += [(i, i + 1), (i + 1, i)]
    return lax.ppermute(array, axis, pairs)


def strip_select():
    lane = lane_ids((LANES, LANES))
    column = lax.broadcasted_iota(jnp.int32, (LANES, LANES), 0)
    chosen = []
    for i in range(STRIP_ROWS):
        at = lane - STRIP * i
        source = jnp.where(at < 3, at + 125, jnp.where(at < 5, at - 3, jnp.where(at < 7, at + 121, at - 7)))
        hit = (source == column) & (at >= 0) & (at < STRIP)
        chosen.append(jnp.where(hit, 1.0, 0.0).astype(BF16))
    return chosen


def whole_strip(mine, got_a, got_b, at, odd):
    from_left = jnp.where(odd, got_a, got_b)
    from_right = jnp.where(odd, got_b, got_a)
    return jnp.where(at < 3, from_left, jnp.where(at < 7, mine, from_right))


def wind_strip_kernel(winds_ref, ra_ref, rb_ref, strip_ref):
    row_odd = lax.axis_index("rows") % 2 == 1
    rows = winds_ref.shape[0]
    chosen = strip_select()
    total = None
    for i in range(STRIP_ROWS):
        y = i - 2
        if 0 <= y < rows:
            line = winds_ref[y].astype(BF16)
        else:
            j = y + HALO if y < 0 else y - rows
            line = jnp.where(row_odd == (y < 0), ra_ref[j], rb_ref[j])
        term = jnp.dot(line, chosen[i], preferred_element_type=F32)
        total = term if total is None else total + term
    strip_ref[...] = total.astype(BF16)


def conc_edge_kernel(conc_ref, mask_ref, a_ref, b_ref):
    odd = lax.axis_index("rows") % 2 == 1
    bins = conc_ref.shape[0] // (mask_ref.shape[0] * (a_ref.shape[1] - 1))
    levels = a_ref.shape[1] - 1
    rows = mask_ref.shape[0]

    def level(k, carry):
        for j in range(HALO):
            upper = conc_ref[pl.ds(k * rows + j, bins, stride=levels * rows), :]
            lower = conc_ref[pl.ds(k * rows + rows - HALO + j, bins, stride=levels * rows), :]
            a_ref[j, k] = jnp.where(odd, upper, lower)
            b_ref[j, k] = jnp.where(odd, lower, upper)
        return carry

    lax.fori_loop(0, levels, level, 0, unroll=4)
    mask = mask_ref[...].astype(F32)
    for j in range(HALO):
        upper = jnp.broadcast_to(mask[j : j + 1], (bins, LANES))
        lower = jnp.broadcast_to(mask[rows - HALO + j : rows - HALO + j + 1], (bins, LANES))
        a_ref[j, levels] = jnp.where(odd, upper, lower)
        b_ref[j, levels] = jnp.where(odd, lower, upper)


def conc_strip_kernel(conc_ref, mask_ref, ra_ref, rb_ref, strip_ref, high_ref, low_ref):
    row_odd = lax.axis_index("rows") % 2 == 1
    levels = ra_ref.shape[1] - 1
    bins = ra_ref.shape[2]
    rows = mask_ref.shape[0]
    mask = mask_ref[...].astype(F32)
    chosen = strip_select()
    total = None
    for i in range(STRIP_ROWS):
        y = i - 2
        for k in range(0, levels + 1, 2):
            pair = []
            for level in (k, min(k + 1, levels)):
                if not 0 <= y < rows:
                    j = y + HALO if y < 0 else y - rows
                    pair.append(jnp.where(row_odd == (y < 0), ra_ref[j, level], rb_ref[j, level]))
                elif level < levels:
                    pair.append(conc_ref[pl.ds(level * rows + y, bins, stride=levels * rows), :])
                else:
                    pair.append(jnp.broadcast_to(mask[y : y + 1], (bins, LANES)))
            both = jnp.concatenate(pair, axis=0)
            high = both.astype(BF16)
            at = slice(k * bins, (k + 2) * bins)
            high_ref[i % 2, at] = high
            low_ref[i % 2, at] = (both - high.astype(F32)).astype(BF16)
        term = jnp.dot(high_ref[i % 2], chosen[i], preferred_element_type=F32) + jnp.dot(
            low_ref[i % 2], chosen[i], preferred_element_type=F32
        )
        total = term if total is None else total + term
    strip_ref[...] = total[: (levels + 1) * bins]


def coefficients(east_w, east, east_e, north_s, north, north_n, valid):
    face_w = 0.5 * (east_w + east)
    face_e = 0.5 * (east + east_e)
    face_s = 0.5 * (north_s + north)
    face_n = 0.5 * (north + north_n)
    out_e = jnp.maximum(face_e, 0.0)
    out_n = jnp.maximum(face_n, 0.0)
    out_w = jnp.minimum(face_w, 0.0)
    out_s = jnp.minimum(face_s, 0.0)
    centre = (1.0 - 4.0 * KAPPA) - (out_e - out_w) - (out_n - out_s)
    west = KAPPA + jnp.maximum(face_w, 0.0)
    east_c = KAPPA - jnp.minimum(face_e, 0.0)
    south = KAPPA + jnp.maximum(face_s, 0.0)
    north_c = KAPPA - jnp.minimum(face_n, 0.0)
    result = (centre, west, east_c, south, north_c)
    return result if valid is None else tuple(jnp.where(valid, c, 0.0) for c in result)


def transport_kernel(
    conc_ref, mask_ref, settle_ref, profile_ref,
    ra_ref, rb_ref, own_ref, ca_ref, cb_ref,
    winds_ref, wra_ref, wrb_ref, wown_ref, wca_ref, wcb_ref,
    out_ref, deposit_ref,
    coef_ref, strip_coef_ref, edge_ref, bound_ref, source_ref, fall_ref,
):
    row, col = lax.axis_index("rows"), lax.axis_index("cols")
    last_row, last_col = lax.axis_size("rows") - 1, lax.axis_size("cols") - 1
    row_odd, col_odd = row % 2 == 1, col % 2 == 1
    levels = ra_ref.shape[1] - 1
    bins = ra_ref.shape[2]
    rows = mask_ref.shape[0]
    tile = (bins, LANES)
    stride = levels * rows

    def halo_of(y, get_a, get_b):
        return jnp.where(row_odd == (y < 0), get_a, get_b)

    def halo_at(y):
        return y + HALO if y < 0 else y - rows

    def wind_row(y):
        if 0 <= y < rows:
            return winds_ref[y]
        j = halo_at(y)
        return halo_of(y, wra_ref[j].astype(F32), wrb_ref[j].astype(F32))

    lanes = lane_ids((levels, LANES))
    at = lanes % STRIP
    wide = lane_ids((2 * levels, LANES)) % STRIP
    strip = whole_strip(
        wown_ref[...].astype(F32), wca_ref[...].astype(F32), wcb_ref[...].astype(F32), wide, col_odd
    )
    strip_u, strip_v = strip[:levels], strip[levels:]
    inside = (
        ((at >= 3) | (col > 0))
        & ((at < 7) | (col < last_col))
        & ((lanes >= 2 * STRIP) | (row > 0))
        & ((lanes < (2 + rows) * STRIP) | (row < last_row))
    )
    found = coefficients(
        roll_lanes(strip_u, 1), strip_u, roll_lanes(strip_u, -1),
        roll_lanes(strip_v, STRIP), strip_v, roll_lanes(strip_v, -STRIP),
        inside,
    )
    for i in range(5):
        strip_coef_ref[i] = found[i]
    for y in range(-2, rows + 2):
        u = wind_row(y)[:levels]
        base = STRIP * (y + 2)
        u_w = jnp.where(lanes == 0, roll_lanes(strip_u, -(base + 2)), roll_lanes(u, 1))
        u_e = jnp.where(
            lanes == LANES - 1, roll_lanes(strip_u, LANES - 1 - (base + 7)), roll_lanes(u, -1)
        )
        valid = None
        if y < 0:
            valid = row > 0
        elif y >= rows:
            valid = row < last_row
        centre, west, east, south, north = coefficients(
            u_w, u, u_e,
            wind_row(y - 1)[levels:], wind_row(y)[levels:], wind_row(y + 1)[levels:],
            valid,
        )
        west = jnp.where(lanes == 0, 0.0, west)
        east = jnp.where(lanes == LANES - 1, 0.0, east)
        for i, c in enumerate((centre, west, east, south, north)):
            coef_ref[5 * (y + 2) + i] = c

    sublanes = lax.broadcasted_iota(jnp.int32, tile, 0)
    settle = jnp.zeros(tile, F32)
    for b in range(bins):
        settle = jnp.where(sublanes == b, settle_ref[b], settle)

    tile_lanes = lane_ids(tile)
    tile_at = tile_lanes % STRIP
    spare = STRIP * STRIP_ROWS

    def edge_of(k):
        at_k = pl.ds(k * bins, bins)
        return whole_strip(own_ref[at_k, :], ca_ref[at_k, :], cb_ref[at_k, :], tile_at, col_odd)

    mask_strip = edge_of(levels)
    zero = jnp.zeros(tile, F32)
    fall_before = [zero] * (STEPS - 1)
    for k in range(levels):
        edge = edge_of(k)
        prof = jnp.broadcast_to(profile_ref[:, k : k + 1], tile)
        parts = []
        rest = prof
        for _ in range(3):
            part = rest.astype(BF16).astype(F32)
            rest = rest - part
            parts.append(part)
        emitted = prof * mask_strip
        c = [jnp.broadcast_to(strip_coef_ref[i, k : k + 1, :], tile) for i in range(5)]
        for step in range(STEPS):
            from_w = c[1] * roll_lanes(edge, 1)
            from_e = c[2] * roll_lanes(edge, -1)
            flow = jnp.where(tile_at == 3, from_w, jnp.where(tile_at == 6, from_e, 0.0))
            for i, part in enumerate(parts):
                flow = jnp.where(tile_lanes == spare + i, part, flow)
            flow = jnp.where(tile_lanes >= spare + 3, 0.0, flow)
            bound_ref[step, k * bins : (k + 1) * bins] = flow
            if step < STEPS - 1:
                fall = settle * edge
                edge = (
                    (c[0] * edge - fall)
                    + (from_w + from_e)
                    + (c[3] * roll_lanes(edge, STRIP) + c[4] * roll_lanes(edge, -STRIP))
                    + (fall_before[step] + emitted)
                )
                fall_before[step] = fall

    lane_of = lax.broadcasted_iota(jnp.int32, (LANES, LANES), 0)
    x_of = lane_ids((LANES, LANES))
    mask = mask_ref[...].astype(F32)
    spread = []
    for y in range(-2, rows + 2):
        base = STRIP * (y + 2)
        hit = ((x_of == 0) & (lane_of == base + 3)) | ((x_of == LANES - 1) & (lane_of == base + 6))
        if 0 <= y < rows:
            line = mask[y : y + 1]
        else:
            j = halo_at(y)
            line = halo_of(y, ra_ref[j, levels], rb_ref[j, levels])[:1]
        emits = (lane_of >= spare) & (lane_of < spare + 3)
        table = jnp.where(hit, 1.0, jnp.where(emits, line, 0.0)).astype(BF16)
        spread.append(jnp.concatenate([table, table], axis=0))
    slot = 0
    slots = {}
    for step in range(STEPS):
        flow = bound_ref[step]
        high = flow.astype(BF16)
        low = (flow - high.astype(F32)).astype(BF16)
        both = jnp.concatenate([high, low], axis=1)
        reach = STEPS - 1 - step
        for y in range(-reach, rows + reach, 2):
            pair = jnp.concatenate([spread[y + 2], spread[y + 3]], axis=1)
            got = jnp.dot(both, pair, preferred_element_type=F32)
            for side in range(2):
                slots[step, y + side] = slot
                source_ref[slot] = got[:, side * LANES : (side + 1) * LANES]
                slot += 1

    fall_ref[...] = jnp.zeros(fall_ref.shape, F32)
    unroll = 8

    def some_levels(trip, carry):
        ks = [trip * unroll + u for u in range(unroll)]

        def start_of(y, k):
            if 0 <= y < rows:
                return conc_ref[pl.ds(k * rows + y, bins, stride=stride), :]
            j = halo_at(y)
            return halo_of(y, ra_ref[j, k], rb_ref[j, k])

        coefs = [{} for _ in ks]
        states = [[{} for _ in range(STEPS + 1)] for _ in ks]
        for u, k in enumerate(ks):
            for y in (-3, -2):
                states[u][0][y] = start_of(y, k)
        for front in range(-2, rows + 4):
            for step in range(STEPS):
                y = front - step
                reach = STEPS - 1 - step
                if not -reach <= y < rows + reach:
                    continue
                index = slots[step, y]
                fall = fall_ref[index]
                for u, k in enumerate(ks):
                    state = states[u][step]
                    if step == 0:
                        state[y + 1] = start_of(y + 1, k)
                        coefs[u][y] = [
                            coef_ref[5 * (y + 2) + i, pl.ds(k, bins, stride=0), :] for i in range(5)
                        ]
                        coefs[u][y][0] = coefs[u][y][0] - settle
                    c = coefs[u][y]
                    a = state[y]
                    source = source_ref[index, pl.ds(k * bins, bins), :] + fall
                    fall = settle * a
                    fresh = (
                        c[0] * a
                        + (c[1] * roll_lanes(a, 1) + c[2] * roll_lanes(a, -1))
                        + (c[3] * state[y - 1] + c[4] * state[y + 1])
                        + source
                    )
                    if step < STEPS - 1:
                        states[u][step + 1][y] = fresh
                    else:
                        out_ref[pl.ds(k * rows + y, bins, stride=stride), :] = fresh
                fall_ref[index] = fall
        return carry

    lax.fori_loop(0, levels // unroll, some_levels, 0)
    for y in range(rows):
        deposit_ref[pl.ds(y, bins, stride=rows), :] = (
            fall_ref[slots[0, y]] + fall_ref[slots[1, y]] + fall_ref[slots[2, y]]
        )


def per_device(conc, nwp, lev_lo, frac, pick, corner_slot, corner_wt, settle, source_mask, profile):
    bins, levels, rows, cols = conc.shape
    peers = pick.shape[2]
    shape = jax.ShapeDtypeStruct
    flat = conc.reshape(bins * levels * rows, cols)

    sent = call(
        select_kernel,
        shape((peers, levels, LANES), BF16),
        (lev_lo.reshape(1, -1), frac.reshape(1, -1), pick.reshape(peers, -1), nwp),
        scratch=(
            pltpu.VMEM((peers, levels, LANES), BF16),
            pltpu.SemaphoreType.DMA((peers // 4,)),
        ),
        out_space=pltpu.HBM,
        flops=2 * 2 * levels * 2048 * 2048,
    )

    flat, sent = lax.optimization_barrier((flat, sent))
    received = lax.all_to_all(sent, "rows", split_axis=0, concat_axis=0, tiled=True)

    edge_rows = shape((HALO, levels + 1, bins, cols), F32)
    ca, cb = call(conc_edge_kernel, (edge_rows, edge_rows), (flat, source_mask), moved=0)
    ra, rb = swap(ca, "rows", True), swap(cb, "rows", False)

    wind_rows = shape((HALO, 2 * levels, cols), BF16)
    winds, wa, wb = call(
        horizontal_kernel,
        (shape((rows, 2 * levels, cols), F32), wind_rows, wind_rows),
        (received, corner_slot, corner_wt),
        scratch=(pltpu.VMEM((2 * levels, peers * LANES // 2), BF16),),
        flops=HIDES,
        limit=20,
    )
    wra, wrb = swap(wa, "rows", True), swap(wb, "rows", False)

    ra, rb, wa = lax.optimization_barrier((ra, rb, wa))
    strips = shape(((levels + 1) * bins, LANES), F32)
    padded = (levels + 2) * bins
    own = call(
        conc_strip_kernel, strips, (flat, source_mask, ra, rb),
        scratch=(pltpu.VMEM((2, padded, LANES), BF16), pltpu.VMEM((2, padded, LANES), BF16)),
        moved=0,
    )
    xa, xb = swap(own, "cols", True), swap(own, "cols", False)
    wown = call(
        wind_strip_kernel, shape((2 * levels, LANES), BF16), (winds, wra, wrb), flops=HIDES
    )
    wxa, wxb = swap(wown, "cols", True), swap(wown, "cols", False)

    tile = (bins, LANES)
    updates = sum(rows + 2 * (STEPS - 1 - s) for s in range(STEPS))
    final, deposit = call(
        transport_kernel,
        (shape(flat.shape, F32), shape((bins * rows, cols), F32)),
        (flat, source_mask, settle, profile, ra, rb, own, xa, xb,
         winds, wra, wrb, wown, wxa, wxb),
        scratch=(
            pltpu.VMEM((5 * (rows + 4), levels, LANES), F32),
            pltpu.VMEM((5, levels, LANES), F32),
            pltpu.VMEM(tile, F32),
            pltpu.VMEM((STEPS, levels * bins, LANES), F32),
            pltpu.VMEM((updates, levels * bins, LANES), F32),
            pltpu.VMEM((updates,) + tile, F32),
        ),
        smem=(2,),
        flops=16 * updates * levels * bins * LANES,
        limit=32,
    )
    return final.reshape(conc.shape), deposit.reshape(bins, rows, cols)


def solution(mesh):
    placed = (
        P(None, None, "rows", "cols"),
        P(None, None, "rows"),
        P(),
        P(),
        P("rows", "cols", None, None),
        P(None, "rows", "cols"),
        P(None, "rows", "cols"),
        P(),
        P("rows", "cols"),
        P(),
    )
    return jax.shard_map(
        per_device,
        mesh=mesh,
        in_specs=placed,
        out_specs=(P(None, None, "rows", "cols"), P(None, "rows", "cols")),
        check_vma=False,
    )
```

```python
import functools

import jax
import jax.numpy as jnp
from jax import lax
from jax.experimental import pallas as pl
from jax.experimental.pallas import tpu as pltpu
from jax.sharding import PartitionSpec as P

STEPS = 3
KAPPA = 0.05
HALO = STEPS
LANES = 128
STRIP = 10
STRIP_ROWS = 12
F32 = jnp.float32
BF16 = jnp.bfloat16
SPLIT = 64
MIB = 1024 * 1024
HIDES = 50_000_000_000


def lane_ids(shape):
    return lax.broadcasted_iota(jnp.int32, shape, len(shape) - 1)


def roll_lanes(x, shift):
    return pltpu.roll(x, shift % LANES, x.ndim - 1)


def call(kernel, out_shape, args, scratch=(), flops=0, smem=(), limit=16, moved=None, out_space=pltpu.VMEM):
    if moved is None:
        moved = sum(a.size * a.dtype.itemsize for a in args) + sum(
            s.size * s.dtype.itemsize for s in jax.tree.leaves(out_shape)
        )
    return pl.pallas_call(
        kernel,
        out_shape=out_shape,
        in_specs=[
            pl.BlockSpec(memory_space=pltpu.SMEM if i in smem else pltpu.VMEM)
            for i in range(len(args))
        ],
        out_specs=jax.tree.map(lambda _: pl.BlockSpec(memory_space=out_space), out_shape),
        scratch_shapes=list(scratch),
        compiler_params=pltpu.CompilerParams(vmem_limit_bytes=limit * MIB),
        cost_estimate=pl.CostEstimate(flops=flops, bytes_accessed=moved, transcendentals=0),
    )(*args)


def select_kernel(lev_ref, frac_ref, pick_ref, nwp_ref, sent_ref, out_ref, sem):
    fields, levels_in, count = nwp_ref.shape
    kept = lev_ref.shape[1]
    ids = lax.broadcasted_iota(jnp.int32, (levels_in, kept), 0)
    low, share = lev_ref[...], frac_ref[...]
    weight = jnp.where(ids == low, 1.0 - share, 0.0) + jnp.where(ids == low + 1, share, 0.0)
    parts = []
    for _ in range(3):
        part = weight.astype(BF16)
        weight = weight - part.astype(F32)
        parts.append(part)
    rows = []
    for field in range(fields):
        mixed = None
        for part in parts:
            term = lax.dot_general(
                part, nwp_ref[field], (((0,), (0,)), ((), ())), preferred_element_type=F32
            )
            mixed = term if mixed is None else mixed + term
        rows.append(mixed.astype(BF16))
    levels = jnp.concatenate(rows, axis=0)
    half = LANES // 2
    width = 2 * LANES
    inner = lax.broadcasted_iota(jnp.int32, (SPLIT, width), 0)
    none = jnp.zeros((SPLIT, width), BF16)
    first = lane_ids((kept, LANES)) < half
    copies = []
    for block in range(pick_ref.shape[0] // 4):
        wanted = jnp.concatenate([pick_ref[4 * block + i : 4 * block + i + 1] for i in range(4)], axis=1)
        group = wanted // SPLIT
        unit = jnp.where(inner == wanted - group * SPLIT, 1.0, 0.0).astype(BF16)
        group = jnp.broadcast_to(group.astype(F32), (SPLIT, width)).astype(BF16)
        hit = jnp.concatenate([jnp.where(group == g, unit, none) for g in range(count // SPLIT)], axis=0)
        got = jnp.dot(levels, hit, preferred_element_type=F32)
        for h in range(2):
            east = got[:kept, h * LANES : (h + 1) * LANES]
            north = got[kept:, h * LANES : (h + 1) * LANES]
            out_ref[4 * block + 2 * h] = jnp.where(first, east, roll_lanes(north, half)).astype(BF16)
            out_ref[4 * block + 2 * h + 1] = jnp.where(
                first, roll_lanes(east, half), north
            ).astype(BF16)
        at = pl.ds(4 * block, 4)
        copies.append(pltpu.make_async_copy(out_ref.at[at], sent_ref.at[at], sem.at[block]))
        copies[-1].start()
    for copy in copies:
        copy.wait()


def corner_tables(slot_ref, wt_ref, count):
    slots = [slot_ref[q] for q in range(4)]
    raw = [wt_ref[q] for q in range(4)]
    total = raw[0] + raw[1] + raw[2] + raw[3]
    norm = [w / total for w in raw]
    groups, units, highs, lows = [], [], [], []
    for q in range(4):
        share = None
        for other in range(4):
            term = jnp.where(slots[q] == slots[other], norm[other], 0.0)
            share = term if share is None else share + term
        for other in range(q):
            share = jnp.where(slots[q] == slots[other], 0.0, share)
        high = share.astype(BF16).astype(F32)
        group = slots[q] // SPLIT
        groups.append(group.astype(F32))
        units.append(slots[q] - group * SPLIT)
        highs.append(high)
        lows.append(share - high)
    inner = lax.broadcasted_iota(jnp.int32, (SPLIT, LANES), 0)
    none = jnp.zeros((SPLIT, LANES), BF16)

    def tables(y):
        line = slice(y, y + 1)
        hits = [inner == units[q][line] for q in range(4)]
        group = [jnp.broadcast_to(groups[q][line], (SPLIT, LANES)).astype(BF16) for q in range(4)]
        result = []
        for parts in (highs, lows):
            own = [jnp.where(hits[q], parts[q][line], 0.0).astype(BF16) for q in range(4)]
            blocks = []
            for g in range(count // SPLIT):
                two = [jnp.where(group[q] == g, own[q], none) for q in range(4)]
                blocks.append((two[0] + two[1]) + (two[2] + two[3]))
            result.append(jnp.concatenate(blocks, axis=0))
        return result

    return tables


def horizontal_kernel(recv_ref, slot_ref, wt_ref, winds_ref, a_ref, b_ref, lev_ref):
    kept = recv_ref.shape[1]
    half = LANES // 2
    first = lane_ids((kept, LANES)) < half
    for pair in range(recv_ref.shape[0] // 2):
        one = recv_ref[2 * pair].astype(F32)
        two = recv_ref[2 * pair + 1].astype(F32)
        at = slice(pair * LANES, (pair + 1) * LANES)
        lev_ref[:kept, at] = jnp.where(first, one, roll_lanes(two, half)).astype(BF16)
        lev_ref[kept:, at] = jnp.where(first, roll_lanes(one, half), two).astype(BF16)
    rows = winds_ref.shape[0]
    lev = lev_ref[...]
    tables = corner_tables(slot_ref, wt_ref, lev_ref.shape[1])
    for y in range(0, rows, 2):
        one, two = tables(y), tables(y + 1)
        got = sum(
            jnp.dot(lev, jnp.concatenate(pair, axis=1), preferred_element_type=F32)
            for pair in zip(one, two)
        )
        winds_ref[y] = got[:, :LANES]
        winds_ref[y + 1] = got[:, LANES:]
    odd = lax.axis_index("rows") % 2 == 1
    for j in range(HALO):
        upper = winds_ref[j]
        lower = winds_ref[rows - HALO + j]
        a_ref[j] = jnp.where(odd, upper, lower).astype(BF16)
        b_ref[j] = jnp.where(odd, lower, upper).astype(BF16)


def swap(array, axis, first):
    peers = lax.axis_size(axis)
    start = 0 if first else 1
    pairs = []
    for i in range(start, peers - 1, 2):
        pairs += [(i, i + 1), (i + 1, i)]
    return lax.ppermute(array, axis, pairs)


def strip_select():
    lane = lane_ids((LANES, LANES))
    column = lax.broadcasted_iota(jnp.int32, (LANES, LANES), 0)
    chosen = []
    for i in range(STRIP_ROWS):
        at = lane - STRIP * i
        source = jnp.where(at < 3, at + 125, jnp.where(at < 5, at - 3, jnp.where(at < 7, at + 121, at - 7)))
        hit = (source == column) & (at >= 0) & (at < STRIP)
        chosen.append(jnp.where(hit, 1.0, 0.0).astype(BF16))
    return chosen


def whole_strip(mine, got_a, got_b, at, odd):
    from_left = jnp.where(odd, got_a, got_b)
    from_right = jnp.where(odd, got_b, got_a)
    return jnp.where(at < 3, from_left, jnp.where(at < 7, mine, from_right))


def side_strip_kernel(winds_ref, ra_ref, rb_ref, conc_ref, strip_ref):
    row_odd = lax.axis_index("rows") % 2 == 1
    rows = winds_ref.shape[0]
    chosen = strip_select()
    total = None
    for i in range(STRIP_ROWS):
        y = i - 2
        if 0 <= y < rows:
            line = winds_ref[y].astype(BF16)
        else:
            j = y + HALO if y < 0 else y - rows
            line = jnp.where(row_odd == (y < 0), ra_ref[j], rb_ref[j])
        term = jnp.dot(line, chosen[i], preferred_element_type=F32)
        total = term if total is None else total + term
    before = conc_ref.shape[0]
    strip_ref[:before] = conc_ref[...]
    strip_ref[before:] = total.astype(BF16)


def conc_edge_kernel(conc_ref, mask_ref, a_ref, b_ref):
    odd = lax.axis_index("rows") % 2 == 1
    bins = a_ref.shape[2] // 2
    pairs = a_ref.shape[1] - 1
    rows = mask_ref.shape[0]
    stride = 2 * pairs * rows

    def pair(p, carry):
        for j in range(HALO):
            upper, lower = (
                jnp.concatenate(
                    [conc_ref[pl.ds((2 * p + h) * rows + y, bins, stride=stride), :] for h in range(2)]
                )
                for y in (j, rows - HALO + j)
            )
            a_ref[j, p] = jnp.where(odd, upper, lower).astype(BF16)
            b_ref[j, p] = jnp.where(odd, lower, upper).astype(BF16)
        return carry

    lax.fori_loop(0, pairs, pair, 0, unroll=4)
    mask = mask_ref[...].astype(F32)
    for j in range(HALO):
        upper = jnp.broadcast_to(mask[j : j + 1], (2 * bins, LANES))
        lower = jnp.broadcast_to(mask[rows - HALO + j : rows - HALO + j + 1], (2 * bins, LANES))
        a_ref[j, pairs] = jnp.where(odd, upper, lower).astype(BF16)
        b_ref[j, pairs] = jnp.where(odd, lower, upper).astype(BF16)


def conc_strip_kernel(conc_ref, mask_ref, ra_ref, rb_ref, strip_ref, line_ref):
    row_odd = lax.axis_index("rows") % 2 == 1
    pairs = ra_ref.shape[1] - 1
    two = ra_ref.shape[2]
    bins = two // 2
    rows = mask_ref.shape[0]
    stride = 2 * pairs * rows
    mask = mask_ref[...].astype(F32)
    chosen = strip_select()
    total = None
    for i in range(STRIP_ROWS):
        y = i - 2
        for p in range(pairs + 1):
            if not 0 <= y < rows:
                j = y + HALO if y < 0 else y - rows
                both = jnp.where(row_odd == (y < 0), ra_ref[j, p], rb_ref[j, p])
            elif p < pairs:
                both = jnp.concatenate(
                    [conc_ref[pl.ds((2 * p + h) * rows + y, bins, stride=stride), :] for h in range(2)]
                ).astype(BF16)
            else:
                both = jnp.broadcast_to(mask[y : y + 1], (two, LANES)).astype(BF16)
            line_ref[i % 2, p * two : (p + 1) * two] = both
        term = jnp.dot(line_ref[i % 2], chosen[i], preferred_element_type=F32)
        total = term if total is None else total + term
    strip_ref[...] = total.astype(BF16)


def coefficients(face_w, face_e, face_s, face_n):
    return (
        (1.0 - 4.0 * KAPPA)
        - (jnp.maximum(face_e, 0.0) - jnp.minimum(face_w, 0.0))
        - (jnp.maximum(face_n, 0.0) - jnp.minimum(face_s, 0.0)),
        KAPPA + jnp.maximum(face_w, 0.0),
        KAPPA - jnp.minimum(face_e, 0.0),
        KAPPA + jnp.maximum(face_s, 0.0),
        KAPPA - jnp.minimum(face_n, 0.0),
    )


def halo_at(y, rows):
    return y + HALO if y < 0 else y - rows


def settle_tile(settle_ref, tile):
    sublanes = lax.broadcasted_iota(jnp.int32, tile, 0)
    settle = jnp.zeros(tile, F32)
    for b in range(tile[0]):
        settle = jnp.where(sublanes == b, settle_ref[b], settle)
    return settle


def first_step_kernel(
    conc_ref, settle_ref, ra_ref, rb_ref, winds_ref, wra_ref, wrb_ref,
    coef_ref, part_ref, deposit_ref, fall_ref,
):
    row, last_row = lax.axis_index("rows"), lax.axis_size("rows") - 1
    row_odd = row % 2 == 1
    levels = coef_ref.shape[1]
    bins = ra_ref.shape[2] // 2
    rows = winds_ref.shape[0]
    tile = (bins, LANES)
    stride = levels * rows

    def wind_row(y):
        if 0 <= y < rows:
            return winds_ref[y]
        j = halo_at(y, rows)
        return jnp.where(row_odd == (y < 0), wra_ref[j].astype(F32), wrb_ref[j].astype(F32))

    lanes = lane_ids((levels, LANES))
    at_west, at_east = lanes == 0, lanes == LANES - 1
    for y in range(-2, rows + 2):
        u = wind_row(y)[:levels]
        north_s, north, north_n = (wind_row(y + d)[levels:] for d in (-1, 0, 1))
        face_w = jnp.where(at_west, 0.0, 0.5 * (roll_lanes(u, 1) + u))
        face_e = jnp.where(at_east, 0.0, 0.5 * (u + roll_lanes(u, -1)))
        found = coefficients(face_w, face_e, 0.5 * (north_s + north), 0.5 * (north + north_n))
        if not 0 <= y < rows:
            valid = row > 0 if y < 0 else row < last_row
            found = [jnp.where(valid, c, 0.0) for c in found]
        found = [
            found[0], jnp.where(at_west, 0.0, found[1]), jnp.where(at_east, 0.0, found[2]), *found[3:]
        ]
        for i in range(5):
            coef_ref[5 * (y + 2) + i] = found[i]

    settle = settle_tile(settle_ref, tile)
    fall_ref[...] = jnp.zeros(fall_ref.shape, F32)
    unroll = 8

    def some_levels(trip, carry):
        ks = [trip * unroll + u for u in range(unroll)]

        def starts_of(y):
            if 0 <= y < rows:
                return [conc_ref[pl.ds(k * rows + y, bins, stride=stride), :] for k in ks]
            j = halo_at(y, rows)
            result = []
            for p in range(unroll // 2):
                at = trip * (unroll // 2) + p
                both = jnp.where(row_odd == (y < 0), ra_ref[j, at].astype(F32), rb_ref[j, at].astype(F32))
                result += [both[:bins], both[bins:]]
            return result

        below, here = starts_of(-3), starts_of(-2)
        for y in range(-2, rows + 2):
            above = starts_of(y + 1)
            fall = fall_ref[y + 2]
            for u, k in enumerate(ks):
                c = [coef_ref[5 * (y + 2) + i, pl.ds(k, bins, stride=0), :] for i in range(5)]
                a = here[u]
                part_ref[y + 2, pl.ds(k * bins, bins), :] = (
                    (c[0] - settle) * a
                    + (c[1] * roll_lanes(a, 1) + c[2] * roll_lanes(a, -1))
                    + (c[3] * below[u] + c[4] * above[u])
                    + fall
                )
                fall = settle * a
            fall_ref[y + 2] = fall
            below, here = here, above
        return carry

    lax.fori_loop(0, levels // unroll, some_levels, 0)
    for y in range(rows):
        deposit_ref[y] = fall_ref[y + 2]


def transport_kernel(
    part_ref, coef_ref, fallen_ref, mask_ref, settle_ref, profile_ref,
    ra_ref, rb_ref, own_ref, xa_ref, xb_ref,
    out_ref, deposit_ref,
    centre_ref, strip_coef_ref, bound_ref, source_ref, fall_ref,
):
    row, col = lax.axis_index("rows"), lax.axis_index("cols")
    last_row, last_col = lax.axis_size("rows") - 1, lax.axis_size("cols") - 1
    row_odd, col_odd = row % 2 == 1, col % 2 == 1
    levels = coef_ref.shape[1]
    two = ra_ref.shape[2]
    bins = two // 2
    rows = mask_ref.shape[0]
    tile = (bins, LANES)
    stride = levels * rows

    def strip_at(start, size):
        at = pl.ds(start, size)
        return whole_strip(
            own_ref[at, :].astype(F32), xa_ref[at, :].astype(F32), xb_ref[at, :].astype(F32),
            lane_ids((size, LANES)) % STRIP, col_odd,
        )

    lanes = lane_ids((levels, LANES))
    at = lanes % STRIP
    winds_at = (levels + 2) * bins
    strip_u, strip_v = strip_at(winds_at, levels), strip_at(winds_at + levels, levels)
    inside = (
        ((at >= 3) | (col > 0))
        & ((at < 7) | (col < last_col))
        & ((lanes >= 2 * STRIP) | (row > 0))
        & ((lanes < (2 + rows) * STRIP) | (row < last_row))
    )
    face_w = 0.5 * (roll_lanes(strip_u, 1) + strip_u)
    face_e = 0.5 * (strip_u + roll_lanes(strip_u, -1))
    found = coefficients(
        face_w, face_e,
        0.5 * (roll_lanes(strip_v, STRIP) + strip_v),
        0.5 * (strip_v + roll_lanes(strip_v, -STRIP)),
    )
    for i in range(5):
        strip_coef_ref[i] = jnp.where(inside, found[i], 0.0)
    sides = jnp.where(at == 3, jnp.minimum(face_w, 0.0), jnp.where(at == 6, -jnp.maximum(face_e, 0.0), 0.0))
    sides = jnp.where(inside, sides, 0.0)
    strip_coef_ref[5] = sides
    for y in range(-1, rows + 1):
        base = STRIP * (y + 2)
        west = roll_lanes(sides, -(base + 3))
        east = roll_lanes(sides, LANES - 1 - (base + 6))
        more = jnp.where(lanes == 0, west, jnp.where(lanes == LANES - 1, east, 0.0))
        centre_ref[y + 1] = coef_ref[5 * (y + 2)] + more

    settle = settle_tile(settle_ref, tile)

    tile_lanes = lane_ids(tile)
    tile_at = tile_lanes % STRIP
    spare = STRIP * STRIP_ROWS
    mask_strip = strip_at(levels * bins, two)[:bins]
    fall_before = [jnp.zeros(tile, F32)] * (STEPS - 1)
    edges = None
    for k in range(levels):
        if k % 2 == 0:
            edges = strip_at(k * bins, two)
        edge = edges[:bins] if k % 2 == 0 else edges[bins:]
        prof = jnp.broadcast_to(profile_ref[:, k : k + 1], tile)
        parts = []
        rest = prof
        for _ in range(3):
            part = rest.astype(BF16).astype(F32)
            rest = rest - part
            parts.append(part)
        emitted = prof * mask_strip
        c = [jnp.broadcast_to(strip_coef_ref[i, k : k + 1, :], tile) for i in range(6)]
        for step in range(STEPS):
            from_w = c[1] * roll_lanes(edge, 1)
            from_e = c[2] * roll_lanes(edge, -1)
            flow = jnp.where(tile_at == 3, from_w, jnp.where(tile_at == 6, from_e, 0.0))
            if step == 0:
                flow = flow + c[5] * edge
            for i, part in enumerate(parts):
                flow = jnp.where(tile_lanes == spare + i, part, flow)
            flow = jnp.where(tile_lanes >= spare + 3, 0.0, flow)
            bound_ref[step, k * bins : (k + 1) * bins] = flow
            if step < STEPS - 1:
                fall = settle * edge
                edge = (
                    (c[0] * edge - fall)
                    + (from_w + from_e)
                    + (c[3] * roll_lanes(edge, STRIP) + c[4] * roll_lanes(edge, -STRIP))
                    + (fall_before[step] + emitted)
                )
                fall_before[step] = fall

    lane_of = lax.broadcasted_iota(jnp.int32, (LANES, LANES), 0)
    x_of = lane_ids((LANES, LANES))
    mask = mask_ref[...].astype(F32)
    last_pair = ra_ref.shape[1] - 1
    spread = []
    for y in range(-2, rows + 2):
        base = STRIP * (y + 2)
        hit = ((x_of == 0) & (lane_of == base + 3)) | ((x_of == LANES - 1) & (lane_of == base + 6))
        if 0 <= y < rows:
            line = mask[y : y + 1]
        else:
            j = halo_at(y, rows)
            line = jnp.where(
                row_odd == (y < 0), ra_ref[j, last_pair].astype(F32), rb_ref[j, last_pair].astype(F32)
            )[:1]
        emits = (lane_of >= spare) & (lane_of < spare + 3)
        table = jnp.where(hit, 1.0, jnp.where(emits, line, 0.0)).astype(BF16)
        spread.append(jnp.concatenate([table, table], axis=0))
    slot = 0
    slots = {}
    for step in range(STEPS):
        flow = bound_ref[step]
        high = flow.astype(BF16)
        low = (flow - high.astype(F32)).astype(BF16)
        both = jnp.concatenate([high, low], axis=1)
        reach = STEPS - 1 - step
        for y in range(-reach, rows + reach, 2):
            pair = jnp.concatenate([spread[y + 2], spread[y + 3]], axis=1)
            got = jnp.dot(both, pair, preferred_element_type=F32)
            for side in range(2):
                slots[step, y + side] = slot
                source_ref[slot] = got[:, side * LANES : (side + 1) * LANES]
                slot += 1

    fall_ref[...] = jnp.zeros(fall_ref.shape, F32)
    unroll = 8
    skipped = slots[1, -1]

    def some_levels(trip, carry):
        ks = [trip * unroll + u for u in range(unroll)]
        coefs = [{} for _ in ks]
        states = [[{} for _ in range(STEPS + 1)] for _ in ks]
        for front in range(-2, rows + 4):
            for step in range(STEPS):
                y = front - step
                reach = STEPS - 1 - step
                if not -reach <= y < rows + reach:
                    continue
                index = slots[step, y]
                if step == 0:
                    for u, k in enumerate(ks):
                        at_k = pl.ds(k * bins, bins)
                        states[u][1][y] = part_ref[y + 2, at_k, :] + source_ref[index, at_k, :]
                    continue
                fall = fall_ref[index - skipped]
                for u, k in enumerate(ks):
                    if step == 1:
                        coefs[u][y] = [centre_ref[y + 1, pl.ds(k, bins, stride=0), :] - settle] + [
                            coef_ref[5 * (y + 2) + i, pl.ds(k, bins, stride=0), :] for i in range(1, 5)
                        ]
                    state = states[u][step]
                    c = coefs[u][y]
                    a = state[y]
                    source = source_ref[index, pl.ds(k * bins, bins), :] + fall
                    fall = settle * a
                    fresh = (
                        c[0] * a
                        + (c[1] * roll_lanes(a, 1) + c[2] * roll_lanes(a, -1))
                        + (c[3] * state[y - 1] + c[4] * state[y + 1])
                        + source
                    )
                    if step < STEPS - 1:
                        states[u][step + 1][y] = fresh
                    else:
                        out_ref[pl.ds(k * rows + y, bins, stride=stride), :] = fresh
                fall_ref[index - skipped] = fall
        return carry

    lax.fori_loop(0, levels // unroll, some_levels, 0)
    for y in range(rows):
        deposit_ref[pl.ds(y, bins, stride=rows), :] = (
            fallen_ref[y] + fall_ref[slots[1, y] - skipped] + fall_ref[slots[2, y] - skipped]
        )


def per_device(conc, nwp, lev_lo, frac, pick, corner_slot, corner_wt, settle, source_mask, profile):
    bins, levels, rows, cols = conc.shape
    peers = pick.shape[2]
    shape = jax.ShapeDtypeStruct
    flat = conc.reshape(bins * levels * rows, cols)

    sent = call(
        select_kernel,
        shape((peers, levels, LANES), BF16),
        (lev_lo.reshape(1, -1), frac.reshape(1, -1), pick.reshape(peers, -1), nwp),
        scratch=(
            pltpu.VMEM((peers, levels, LANES), BF16),
            pltpu.SemaphoreType.DMA((peers // 4,)),
        ),
        out_space=pltpu.HBM,
        flops=2 * 2 * levels * 2048 * 2048,
    )

    flat, sent = lax.optimization_barrier((flat, sent))
    received = lax.all_to_all(sent, "rows", split_axis=0, concat_axis=0, tiled=True)

    pairs = levels // 2 + 1
    edge_rows = shape((HALO, pairs, 2 * bins, cols), BF16)
    ca, cb = call(conc_edge_kernel, (edge_rows, edge_rows), (flat, source_mask), moved=0)
    ra, rb = swap(ca, "rows", True), swap(cb, "rows", False)

    wind_rows = shape((HALO, 2 * levels, cols), BF16)
    winds, wa, wb = call(
        horizontal_kernel,
        (shape((rows, 2 * levels, cols), F32), wind_rows, wind_rows),
        (received, corner_slot, corner_wt),
        scratch=(pltpu.VMEM((2 * levels, peers * LANES // 2), BF16),),
        flops=HIDES,
        limit=20,
    )
    wra, wrb = swap(wa, "rows", True), swap(wb, "rows", False)

    ra, rb, wa = lax.optimization_barrier((ra, rb, wa))
    strips = shape((pairs * 2 * bins, LANES), BF16)
    conc_strip = call(
        conc_strip_kernel, strips, (flat, source_mask, ra, rb),
        scratch=(pltpu.VMEM((2, pairs * 2 * bins, LANES), BF16),),
        moved=0,
    )
    own = call(
        side_strip_kernel,
        shape((pairs * 2 * bins + 2 * levels, LANES), BF16),
        (winds, wra, wrb, conc_strip),
        flops=HIDES,
    )
    xa, xb = swap(own, "cols", True), swap(own, "cols", False)

    tile = (bins, LANES)
    part, coef, fallen = (
        shape((rows + 4, levels * bins, LANES), F32),
        shape((5 * (rows + 4), levels, LANES), F32),
        shape((rows,) + tile, F32),
    )
    coef, part, fallen = call(
        first_step_kernel,
        (coef, part, fallen),
        (flat, settle, ra, rb, winds, wra, wrb),
        scratch=(pltpu.VMEM((rows + 4,) + tile, F32),),
        smem=(1,),
        moved=0,
    )
    updates = sum(rows + 2 * (STEPS - 1 - s) for s in range(STEPS))
    final, deposit = call(
        transport_kernel,
        (shape(flat.shape, F32), shape((bins * rows, cols), F32)),
        (part, coef, fallen, source_mask, settle, profile, ra, rb, own, xa, xb),
        scratch=(
            pltpu.VMEM((rows + 2, levels, LANES), F32),
            pltpu.VMEM((6, levels, LANES), F32),
            pltpu.VMEM((STEPS, levels * bins, LANES), F32),
            pltpu.VMEM((updates, levels * bins, LANES), F32),
            pltpu.VMEM((updates - rows - 4,) + tile, F32),
        ),
        smem=(4,),
        flops=16 * updates * levels * bins * LANES,
        limit=24,
    )
    return final.reshape(conc.shape), deposit.reshape(bins, rows, cols)


def solution(mesh):
    placed = (
        P(None, None, "rows", "cols"),
        P(None, None, "rows"),
        P(),
        P(),
        P("rows", "cols", None, None),
        P(None, "rows", "cols"),
        P(None, "rows", "cols"),
        P(),
        P("rows", "cols"),
        P(),
    )
    return jax.shard_map(
        per_device,
        mesh=mesh,
        in_specs=placed,
        out_specs=(P(None, None, "rows", "cols"), P(None, "rows", "cols")),
        check_vma=False,
    )
```

```python
import functools

import jax
import jax.numpy as jnp
from jax import lax
from jax.experimental import pallas as pl
from jax.experimental.pallas import tpu as pltpu
from jax.sharding import PartitionSpec as P

STEPS = 3
KAPPA = 0.05
HALO = STEPS
LANES = 128
STRIP = 10
STRIP_ROWS = 12
F32 = jnp.float32
BF16 = jnp.bfloat16
SPLIT = 64
MIB = 1024 * 1024
HIDES = 50_000_000_000


def lane_ids(shape):
    return lax.broadcasted_iota(jnp.int32, shape, len(shape) - 1)


def roll_lanes(x, shift):
    return pltpu.roll(x, shift % LANES, x.ndim - 1)


def call(kernel, out_shape, args, scratch=(), flops=0, smem=(), limit=16, moved=None, out_spaces=None):
    if moved is None:
        moved = sum(a.size * a.dtype.itemsize for a in args) + sum(
            s.size * s.dtype.itemsize for s in jax.tree.leaves(out_shape)
        )
    leaves, tree = jax.tree.flatten(out_shape)
    spaces = out_spaces or (pltpu.VMEM,) * len(leaves)
    return pl.pallas_call(
        kernel,
        out_shape=out_shape,
        in_specs=[
            pl.BlockSpec(memory_space=pltpu.SMEM if i in smem else pltpu.VMEM)
            for i in range(len(args))
        ],
        out_specs=jax.tree.unflatten(tree, [pl.BlockSpec(memory_space=m) for m in spaces]),
        scratch_shapes=list(scratch),
        compiler_params=pltpu.CompilerParams(vmem_limit_bytes=limit * MIB),
        cost_estimate=pl.CostEstimate(flops=flops, bytes_accessed=moved, transcendentals=0),
    )(*args)


def one_hot(wanted, count):
    width = wanted.shape[1]
    group = wanted // SPLIT
    place = lax.broadcasted_iota(jnp.int32, (SPLIT, width), 0)
    unit = jnp.where(place == wanted - group * SPLIT, 1.0, 0.0).astype(BF16)
    none = jnp.zeros((SPLIT, width), BF16)
    group = jnp.broadcast_to(group.astype(F32), (SPLIT, width)).astype(BF16)
    return jnp.concatenate([jnp.where(group == g, unit, none) for g in range(count // SPLIT)], axis=0)


def select_kernel(lev_ref, frac_ref, pick_ref, nwp_ref, sent_ref, out_ref, sem):
    fields, levels_in, count = nwp_ref.shape
    kept = lev_ref.shape[1]
    ids = lax.broadcasted_iota(jnp.int32, (levels_in, kept), 0)
    low, share = lev_ref[...], frac_ref[...]
    weight = jnp.where(ids == low, 1.0 - share, 0.0) + jnp.where(ids == low + 1, share, 0.0)
    parts = []
    for _ in range(3):
        part = weight.astype(BF16)
        weight = weight - part.astype(F32)
        parts.append(part)
    stacked = jnp.concatenate(parts, axis=1)
    rows = []
    for field in range(fields):
        mixed = lax.dot_general(
            stacked, nwp_ref[field], (((0,), (0,)), ((), ())), preferred_element_type=F32
        )
        rows.append((mixed[:kept] + mixed[kept : 2 * kept] + mixed[2 * kept :]).astype(BF16))
    levels = jnp.concatenate(rows, axis=0)
    half = LANES // 2
    width = 2 * LANES
    first = lane_ids((kept, LANES)) < half
    copies = []
    for block in range(pick_ref.shape[0] // 4):
        wanted = jnp.concatenate([pick_ref[4 * block + i : 4 * block + i + 1] for i in range(4)], axis=1)
        hit = one_hot(wanted, count)
        got = jnp.dot(levels, hit, preferred_element_type=F32)
        for h in range(2):
            east = got[:kept, h * LANES : (h + 1) * LANES]
            north = got[kept:, h * LANES : (h + 1) * LANES]
            out_ref[4 * block + 2 * h] = jnp.where(first, east, roll_lanes(north, half)).astype(BF16)
            out_ref[4 * block + 2 * h + 1] = jnp.where(
                first, roll_lanes(east, half), north
            ).astype(BF16)
        at = pl.ds(4 * block, 4)
        copies.append(pltpu.make_async_copy(out_ref.at[at], sent_ref.at[at], sem.at[block]))
        copies[-1].start()
    for copy in copies:
        copy.wait()


def horizontal_kernel(recv_ref, slot_ref, wt_ref, winds_ref, a_ref, b_ref, lev_ref):
    kept = recv_ref.shape[1]
    half = LANES // 2
    first = lane_ids((kept, LANES)) < half
    for pair in range(recv_ref.shape[0] // 2):
        one = recv_ref[2 * pair].astype(F32)
        two = recv_ref[2 * pair + 1].astype(F32)
        at = slice(pair * LANES, (pair + 1) * LANES)
        lev_ref[:kept, at] = jnp.where(first, one, roll_lanes(two, half)).astype(BF16)
        lev_ref[kept:, at] = jnp.where(first, roll_lanes(one, half), two).astype(BF16)
    rows = winds_ref.shape[0]
    lev = lev_ref[...]
    raw = [wt_ref[q] for q in range(4)]
    total = raw[0] + raw[1] + raw[2] + raw[3]
    norm = [w / total for w in raw]
    for y in range(0, rows, 2):
        winds = [None, None]
        for q in range(4):
            wanted = jnp.concatenate([slot_ref[q, y + h : y + h + 1] for h in range(2)], axis=1)
            got = jnp.dot(lev, one_hot(wanted, lev_ref.shape[1]), preferred_element_type=F32)
            for h in range(2):
                term = norm[q][y + h : y + h + 1] * got[:, h * LANES : (h + 1) * LANES]
                winds[h] = term if winds[h] is None else winds[h] + term
        winds_ref[y] = winds[0]
        winds_ref[y + 1] = winds[1]
    odd = lax.axis_index("rows") % 2 == 1
    for j in range(HALO):
        upper = winds_ref[j]
        lower = winds_ref[rows - HALO + j]
        a_ref[j] = jnp.where(odd, upper, lower).astype(BF16)
        b_ref[j] = jnp.where(odd, lower, upper).astype(BF16)


def swap(array, axis, first):
    peers = lax.axis_size(axis)
    start = 0 if first else 1
    pairs = []
    for i in range(start, peers - 1, 2):
        pairs += [(i, i + 1), (i + 1, i)]
    return lax.ppermute(array, axis, pairs)


def strip_select():
    lane = lane_ids((LANES, LANES))
    column = lax.broadcasted_iota(jnp.int32, (LANES, LANES), 0)
    chosen = []
    for i in range(STRIP_ROWS):
        at = lane - STRIP * i
        source = jnp.where(at < 3, at + 125, jnp.where(at < 5, at - 3, jnp.where(at < 7, at + 121, at - 7)))
        hit = (source == column) & (at >= 0) & (at < STRIP)
        chosen.append(jnp.where(hit, 1.0, 0.0).astype(BF16))
    return chosen


def whole_strip(mine, got_a, got_b, at, odd):
    from_left = jnp.where(odd, got_a, got_b)
    from_right = jnp.where(odd, got_b, got_a)
    return jnp.where(at < 3, from_left, jnp.where(at < 7, mine, from_right))


def side_strip_kernel(winds_ref, ra_ref, rb_ref, conc_ref, strip_ref):
    row_odd = lax.axis_index("rows") % 2 == 1
    rows = winds_ref.shape[0]
    chosen = strip_select()
    total = None
    for i in range(STRIP_ROWS):
        y = i - 2
        if 0 <= y < rows:
            line = winds_ref[y].astype(BF16)
        else:
            j = y + HALO if y < 0 else y - rows
            line = jnp.where(row_odd == (y < 0), ra_ref[j], rb_ref[j])
        term = jnp.dot(line, chosen[i], preferred_element_type=F32)
        total = term if total is None else total + term
    before = conc_ref.shape[0]
    strip_ref[:before] = conc_ref[...]
    strip_ref[before:] = total.astype(BF16)


def conc_edge_kernel(conc_ref, mask_ref, a_ref, b_ref):
    odd = lax.axis_index("rows") % 2 == 1
    bins = a_ref.shape[2] // 2
    pairs = a_ref.shape[1] - 1
    rows = mask_ref.shape[0]
    stride = 2 * pairs * rows

    def pair(p, carry):
        for j in range(HALO):
            upper, lower = (
                jnp.concatenate(
                    [conc_ref[pl.ds((2 * p + h) * rows + y, bins, stride=stride), :] for h in range(2)]
                )
                for y in (j, rows - HALO + j)
            )
            a_ref[j, p] = jnp.where(odd, upper, lower).astype(BF16)
            b_ref[j, p] = jnp.where(odd, lower, upper).astype(BF16)
        return carry

    lax.fori_loop(0, pairs, pair, 0, unroll=4)
    mask = mask_ref[...].astype(F32)
    for j in range(HALO):
        upper = jnp.broadcast_to(mask[j : j + 1], (2 * bins, LANES))
        lower = jnp.broadcast_to(mask[rows - HALO + j : rows - HALO + j + 1], (2 * bins, LANES))
        a_ref[j, pairs] = jnp.where(odd, upper, lower).astype(BF16)
        b_ref[j, pairs] = jnp.where(odd, lower, upper).astype(BF16)


def conc_strip_kernel(conc_ref, mask_ref, ra_ref, rb_ref, strip_ref, line_ref):
    row_odd = lax.axis_index("rows") % 2 == 1
    pairs = ra_ref.shape[1] - 1
    two = ra_ref.shape[2]
    bins = two // 2
    rows = mask_ref.shape[0]
    stride = 2 * pairs * rows
    mask = mask_ref[...].astype(F32)
    chosen = strip_select()
    total = None
    for i in range(STRIP_ROWS):
        y = i - 2
        for p in range(pairs + 1):
            if not 0 <= y < rows:
                j = y + HALO if y < 0 else y - rows
                both = jnp.where(row_odd == (y < 0), ra_ref[j, p], rb_ref[j, p])
            elif p < pairs:
                both = jnp.concatenate(
                    [conc_ref[pl.ds((2 * p + h) * rows + y, bins, stride=stride), :] for h in range(2)]
                ).astype(BF16)
            else:
                both = jnp.broadcast_to(mask[y : y + 1], (two, LANES)).astype(BF16)
            line_ref[i % 2, p * two : (p + 1) * two] = both
        term = jnp.dot(line_ref[i % 2], chosen[i], preferred_element_type=F32)
        total = term if total is None else total + term
    strip_ref[...] = total.astype(BF16)


def coefficients(face_w, face_e, face_s, face_n):
    return (
        (1.0 - 4.0 * KAPPA)
        - (jnp.maximum(face_e, 0.0) - jnp.minimum(face_w, 0.0))
        - (jnp.maximum(face_n, 0.0) - jnp.minimum(face_s, 0.0)),
        KAPPA + jnp.maximum(face_w, 0.0),
        KAPPA - jnp.minimum(face_e, 0.0),
        KAPPA + jnp.maximum(face_s, 0.0),
        KAPPA - jnp.minimum(face_n, 0.0),
    )


def halo_at(y, rows):
    return y + HALO if y < 0 else y - rows


def settle_tile(settle_ref, tile):
    sublanes = lax.broadcasted_iota(jnp.int32, tile, 0)
    settle = jnp.zeros(tile, F32)
    for b in range(tile[0]):
        settle = jnp.where(sublanes == b, settle_ref[b], settle)
    return settle


def first_step_kernel(
    conc_ref, settle_ref, ra_ref, rb_ref, winds_ref, wra_ref, wrb_ref,
    coef_ref, part_ref, deposit_ref, fall_ref,
):
    row, last_row = lax.axis_index("rows"), lax.axis_size("rows") - 1
    row_odd = row % 2 == 1
    levels = coef_ref.shape[1]
    bins = ra_ref.shape[2] // 2
    rows = winds_ref.shape[0]
    tile = (bins, LANES)
    stride = levels * rows

    def wind_row(y):
        if 0 <= y < rows:
            return winds_ref[y]
        j = halo_at(y, rows)
        return jnp.where(row_odd == (y < 0), wra_ref[j].astype(F32), wrb_ref[j].astype(F32))

    lanes = lane_ids((levels, LANES))
    at_west, at_east = lanes == 0, lanes == LANES - 1
    for y in range(-2, rows + 2):
        u = wind_row(y)[:levels]
        north_s, north, north_n = (wind_row(y + d)[levels:] for d in (-1, 0, 1))
        face_w = jnp.where(at_west, 0.0, 0.5 * (roll_lanes(u, 1) + u))
        face_e = jnp.where(at_east, 0.0, 0.5 * (u + roll_lanes(u, -1)))
        found = coefficients(face_w, face_e, 0.5 * (north_s + north), 0.5 * (north + north_n))
        if not 0 <= y < rows:
            valid = row > 0 if y < 0 else row < last_row
            found = [jnp.where(valid, c, 0.0) for c in found]
        found = [
            found[0], jnp.where(at_west, 0.0, found[1]), jnp.where(at_east, 0.0, found[2]), *found[3:]
        ]
        for i in range(5):
            coef_ref[5 * (y + 2) + i] = found[i]

    settle = settle_tile(settle_ref, tile)
    fall_ref[...] = jnp.zeros(fall_ref.shape, F32)
    unroll = 8

    def some_levels(trip, carry):
        ks = [trip * unroll + u for u in range(unroll)]

        def starts_of(y):
            if 0 <= y < rows:
                return [conc_ref[pl.ds(k * rows + y, bins, stride=stride), :] for k in ks]
            j = halo_at(y, rows)
            result = []
            for p in range(unroll // 2):
                at = trip * (unroll // 2) + p
                both = jnp.where(row_odd == (y < 0), ra_ref[j, at].astype(F32), rb_ref[j, at].astype(F32))
                result += [both[:bins], both[bins:]]
            return result

        below, here = starts_of(-3), starts_of(-2)
        for y in range(-2, rows + 2):
            above = starts_of(y + 1)
            fall = fall_ref[y + 2]
            for u, k in enumerate(ks):
                c = [coef_ref[5 * (y + 2) + i, pl.ds(k, bins, stride=0), :] for i in range(5)]
                a = here[u]
                part_ref[y + 2, pl.ds(k * bins, bins), :] = (
                    (c[0] - settle) * a
                    + (c[1] * roll_lanes(a, 1) + c[2] * roll_lanes(a, -1))
                    + (c[3] * below[u] + c[4] * above[u])
                    + fall
                )
                fall = settle * a
            fall_ref[y + 2] = fall
            below, here = here, above
        return carry

    lax.fori_loop(0, levels // unroll, some_levels, 0)
    for y in range(rows):
        deposit_ref[y] = fall_ref[y + 2]


def transport_kernel(
    part_ref, coef_ref, fallen_ref, mask_ref, settle_ref, profile_ref,
    ra_ref, rb_ref, own_ref, xa_ref, xb_ref,
    out_ref, deposit_ref,
    centre_ref, strip_coef_ref, bound_ref, source_ref, fall_ref,
):
    row, col = lax.axis_index("rows"), lax.axis_index("cols")
    last_row, last_col = lax.axis_size("rows") - 1, lax.axis_size("cols") - 1
    row_odd, col_odd = row % 2 == 1, col % 2 == 1
    levels = coef_ref.shape[1]
    two = ra_ref.shape[2]
    bins = two // 2
    rows = mask_ref.shape[0]
    tile = (bins, LANES)
    stride = levels * rows

    def strip_at(start, size):
        at = pl.ds(start, size)
        return whole_strip(
            own_ref[at, :].astype(F32), xa_ref[at, :].astype(F32), xb_ref[at, :].astype(F32),
            lane_ids((size, LANES)) % STRIP, col_odd,
        )

    lanes = lane_ids((levels, LANES))
    at = lanes % STRIP
    winds_at = (levels + 2) * bins
    strip_u, strip_v = strip_at(winds_at, levels), strip_at(winds_at + levels, levels)
    inside = (
        ((at >= 3) | (col > 0))
        & ((at < 7) | (col < last_col))
        & ((lanes >= 2 * STRIP) | (row > 0))
        & ((lanes < (2 + rows) * STRIP) | (row < last_row))
    )
    face_w = 0.5 * (roll_lanes(strip_u, 1) + strip_u)
    face_e = 0.5 * (strip_u + roll_lanes(strip_u, -1))
    found = coefficients(
        face_w, face_e,
        0.5 * (roll_lanes(strip_v, STRIP) + strip_v),
        0.5 * (strip_v + roll_lanes(strip_v, -STRIP)),
    )
    for i in range(5):
        strip_coef_ref[i] = jnp.where(inside, found[i], 0.0)
    sides = jnp.where(at == 3, jnp.minimum(face_w, 0.0), jnp.where(at == 6, -jnp.maximum(face_e, 0.0), 0.0))
    sides = jnp.where(inside, sides, 0.0)
    strip_coef_ref[5] = sides
    for y in range(-1, rows + 1):
        base = STRIP * (y + 2)
        west = roll_lanes(sides, -(base + 3))
        east = roll_lanes(sides, LANES - 1 - (base + 6))
        more = jnp.where(lanes == 0, west, jnp.where(lanes == LANES - 1, east, 0.0))
        centre_ref[y + 1] = coef_ref[5 * (y + 2)] + more

    settle = settle_tile(settle_ref, tile)

    tile_lanes = lane_ids(tile)
    tile_at = tile_lanes % STRIP
    spare = STRIP * STRIP_ROWS
    mask_strip = strip_at(levels * bins, two)[:bins]
    fall_before = [jnp.zeros(tile, F32)] * (STEPS - 1)
    edges = None
    for k in range(levels):
        if k % 2 == 0:
            edges = strip_at(k * bins, two)
        edge = edges[:bins] if k % 2 == 0 else edges[bins:]
        prof = jnp.broadcast_to(profile_ref[:, k : k + 1], tile)
        parts = []
        rest = prof
        for _ in range(3):
            part = rest.astype(BF16).astype(F32)
            rest = rest - part
            parts.append(part)
        emitted = prof * mask_strip
        c = [jnp.broadcast_to(strip_coef_ref[i, k : k + 1, :], tile) for i in range(6)]
        for step in range(STEPS):
            from_w = c[1] * roll_lanes(edge, 1)
            from_e = c[2] * roll_lanes(edge, -1)
            flow = jnp.where(tile_at == 3, from_w, jnp.where(tile_at == 6, from_e, 0.0))
            if step == 0:
                flow = flow + c[5] * edge
            for i, part in enumerate(parts):
                flow = jnp.where(tile_lanes == spare + i, part, flow)
            flow = jnp.where(tile_lanes >= spare + 3, 0.0, flow)
            bound_ref[step, k * bins : (k + 1) * bins] = flow
            if step < STEPS - 1:
                fall = settle * edge
                edge = (
                    (c[0] * edge - fall)
                    + (from_w + from_e)
                    + (c[3] * roll_lanes(edge, STRIP) + c[4] * roll_lanes(edge, -STRIP))
                    + (fall_before[step] + emitted)
                )
                fall_before[step] = fall

    lane_of = lax.broadcasted_iota(jnp.int32, (LANES, LANES), 0)
    x_of = lane_ids((LANES, LANES))
    mask = mask_ref[...].astype(F32)
    last_pair = ra_ref.shape[1] - 1
    spread = []
    for y in range(-2, rows + 2):
        base = STRIP * (y + 2)
        hit = ((x_of == 0) & (lane_of == base + 3)) | ((x_of == LANES - 1) & (lane_of == base + 6))
        if 0 <= y < rows:
            line = mask[y : y + 1]
        else:
            j = halo_at(y, rows)
            line = jnp.where(
                row_odd == (y < 0), ra_ref[j, last_pair].astype(F32), rb_ref[j, last_pair].astype(F32)
            )[:1]
        emits = (lane_of >= spare) & (lane_of < spare + 3)
        table = jnp.where(hit, 1.0, jnp.where(emits, line, 0.0)).astype(BF16)
        spread.append(jnp.concatenate([table, table], axis=0))
    slot = 0
    slots = {}
    for step in range(STEPS):
        flow = bound_ref[step]
        high = flow.astype(BF16)
        low = (flow - high.astype(F32)).astype(BF16)
        both = jnp.concatenate([high, low], axis=1)
        reach = STEPS - 1 - step
        for y in range(-reach, rows + reach, 2):
            pair = jnp.concatenate([spread[y + 2], spread[y + 3]], axis=1)
            got = jnp.dot(both, pair, preferred_element_type=F32)
            for side in range(2):
                slots[step, y + side] = slot
                source_ref[slot] = got[:, side * LANES : (side + 1) * LANES]
                slot += 1

    fall_ref[...] = jnp.zeros(fall_ref.shape, F32)
    unroll = 8
    skipped = slots[1, -1]

    def some_levels(trip, carry):
        ks = [trip * unroll + u for u in range(unroll)]
        coefs = [{} for _ in ks]
        states = [[{} for _ in range(STEPS + 1)] for _ in ks]
        for front in range(-2, rows + 4):
            for step in range(STEPS):
                y = front - step
                reach = STEPS - 1 - step
                if not -reach <= y < rows + reach:
                    continue
                index = slots[step, y]
                if step == 0:
                    for u, k in enumerate(ks):
                        at_k = pl.ds(k * bins, bins)
                        states[u][1][y] = part_ref[y + 2, at_k, :] + source_ref[index, at_k, :]
                    continue
                fall = fall_ref[index - skipped]
                for u, k in enumerate(ks):
                    if step == 1:
                        coefs[u][y] = [centre_ref[y + 1, pl.ds(k, bins, stride=0), :] - settle] + [
                            coef_ref[5 * (y + 2) + i, pl.ds(k, bins, stride=0), :] for i in range(1, 5)
                        ]
                    state = states[u][step]
                    c = coefs[u][y]
                    a = state[y]
                    source = source_ref[index, pl.ds(k * bins, bins), :] + fall
                    fall = settle * a
                    fresh = (
                        c[0] * a
                        + (c[1] * roll_lanes(a, 1) + c[2] * roll_lanes(a, -1))
                        + (c[3] * state[y - 1] + c[4] * state[y + 1])
                        + source
                    )
                    if step < STEPS - 1:
                        states[u][step + 1][y] = fresh
                    else:
                        out_ref[pl.ds(k * rows + y, bins, stride=stride), :] = fresh
                fall_ref[index - skipped] = fall
        return carry

    lax.fori_loop(0, levels // unroll, some_levels, 0)
    for y in range(rows):
        deposit_ref[pl.ds(y, bins, stride=rows), :] = (
            fallen_ref[y] + fall_ref[slots[1, y] - skipped] + fall_ref[slots[2, y] - skipped]
        )


def per_device(conc, nwp, lev_lo, frac, pick, corner_slot, corner_wt, settle, source_mask, profile):
    bins, levels, rows, cols = conc.shape
    peers = pick.shape[2]
    shape = jax.ShapeDtypeStruct
    flat = conc.reshape(bins * levels * rows, cols)

    sent = call(
        select_kernel,
        shape((peers, levels, LANES), BF16),
        (lev_lo.reshape(1, -1), frac.reshape(1, -1), pick.reshape(peers, -1), nwp),
        scratch=(
            pltpu.VMEM((peers, levels, LANES), BF16),
            pltpu.SemaphoreType.DMA((peers // 4,)),
        ),
        out_spaces=(pltpu.HBM,),
        flops=2 * 2 * levels * 2048 * 2048,
    )

    flat, sent = lax.optimization_barrier((flat, sent))
    received = lax.all_to_all(sent, "rows", split_axis=0, concat_axis=0, tiled=True)

    pairs = levels // 2 + 1
    edge_rows = shape((HALO, pairs, 2 * bins, cols), BF16)
    ca, cb = call(conc_edge_kernel, (edge_rows, edge_rows), (flat, source_mask), moved=0)
    ra, rb = swap(ca, "rows", True), swap(cb, "rows", False)

    wind_rows = shape((HALO, 2 * levels, cols), BF16)
    winds, wa, wb = call(
        horizontal_kernel,
        (shape((rows, 2 * levels, cols), F32), wind_rows, wind_rows),
        (received, corner_slot, corner_wt),
        scratch=(pltpu.VMEM((2 * levels, peers * LANES // 2), BF16),),
        flops=HIDES,
        limit=20,
    )
    wra, wrb = swap(wa, "rows", True), swap(wb, "rows", False)

    ra, rb, wa = lax.optimization_barrier((ra, rb, wa))
    strips = shape((pairs * 2 * bins, LANES), BF16)
    conc_strip = call(
        conc_strip_kernel, strips, (flat, source_mask, ra, rb),
        scratch=(pltpu.VMEM((2, pairs * 2 * bins, LANES), BF16),),
        moved=0,
    )
    own = call(
        side_strip_kernel,
        shape((pairs * 2 * bins + 2 * levels, LANES), BF16),
        (winds, wra, wrb, conc_strip),
        flops=HIDES,
    )
    xa, xb = swap(own, "cols", True), swap(own, "cols", False)

    tile = (bins, LANES)
    part, coef, fallen = (
        shape((rows + 4, levels * bins, LANES), F32),
        shape((5 * (rows + 4), levels, LANES), F32),
        shape((rows,) + tile, F32),
    )
    coef, part, fallen = call(
        first_step_kernel,
        (coef, part, fallen),
        (flat, settle, ra, rb, winds, wra, wrb),
        scratch=(pltpu.VMEM((rows + 4,) + tile, F32),),
        smem=(1,),
        moved=0,
    )
    updates = sum(rows + 2 * (STEPS - 1 - s) for s in range(STEPS))
    final, deposit = call(
        transport_kernel,
        (shape(flat.shape, F32), shape((bins * rows, cols), F32)),
        (part, coef, fallen, source_mask, settle, profile, ra, rb, own, xa, xb),
        scratch=(
            pltpu.VMEM((rows + 2, levels, LANES), F32),
            pltpu.VMEM((6, levels, LANES), F32),
            pltpu.VMEM((STEPS, levels * bins, LANES), F32),
            pltpu.VMEM((updates, levels * bins, LANES), F32),
            pltpu.VMEM((updates - rows - 4,) + tile, F32),
        ),
        smem=(4,),
        flops=16 * updates * levels * bins * LANES,
        limit=24,
    )
    return final.reshape(conc.shape), deposit.reshape(bins, rows, cols)


def solution(mesh):
    placed = (
        P(None, None, "rows", "cols"),
        P(None, None, "rows"),
        P(),
        P(),
        P("rows", "cols", None, None),
        P(None, "rows", "cols"),
        P(None, "rows", "cols"),
        P(),
        P("rows", "cols"),
        P(),
    )
    return jax.shard_map(
        per_device,
        mesh=mesh,
        in_specs=placed,
        out_specs=(P(None, None, "rows", "cols"), P(None, "rows", "cols")),
        check_vma=False,
    )
```

```python
import functools

import jax
import jax.numpy as jnp
from jax import lax
from jax.experimental import pallas as pl
from jax.experimental.pallas import tpu as pltpu
from jax.sharding import PartitionSpec as P

STEPS = 3
KAPPA = 0.05
HALO = STEPS
LANES = 128
STRIP = 10
STRIP_ROWS = 12
F32 = jnp.float32
BF16 = jnp.bfloat16
SPLIT = 64
MIB = 1024 * 1024
HIDES = 50_000_000_000


def lane_ids(shape):
    return lax.broadcasted_iota(jnp.int32, shape, len(shape) - 1)


def roll_lanes(x, shift):
    return pltpu.roll(x, shift % LANES, x.ndim - 1)


def call(kernel, out_shape, args, scratch=(), flops=0, smem=(), limit=16, moved=None, out_spaces=None):
    if moved is None:
        moved = sum(a.size * a.dtype.itemsize for a in args) + sum(
            s.size * s.dtype.itemsize for s in jax.tree.leaves(out_shape)
        )
    leaves, tree = jax.tree.flatten(out_shape)
    spaces = out_spaces or (pltpu.VMEM,) * len(leaves)
    return pl.pallas_call(
        kernel,
        out_shape=out_shape,
        in_specs=[
            pl.BlockSpec(memory_space=pltpu.SMEM if i in smem else pltpu.VMEM)
            for i in range(len(args))
        ],
        out_specs=jax.tree.unflatten(tree, [pl.BlockSpec(memory_space=m) for m in spaces]),
        scratch_shapes=list(scratch),
        compiler_params=pltpu.CompilerParams(vmem_limit_bytes=limit * MIB),
        cost_estimate=pl.CostEstimate(flops=flops, bytes_accessed=moved, transcendentals=0),
    )(*args)


def one_hot(wanted, count):
    width = wanted.shape[1]
    group = wanted // SPLIT
    place = lax.broadcasted_iota(jnp.int32, (SPLIT, width), 0)
    unit = jnp.where(place == wanted - group * SPLIT, 1.0, 0.0).astype(BF16)
    none = jnp.zeros((SPLIT, width), BF16)
    group = jnp.broadcast_to(group.astype(F32), (SPLIT, width)).astype(BF16)
    return jnp.concatenate([jnp.where(group == g, unit, none) for g in range(count // SPLIT)], axis=0)


def select_kernel(lev_ref, frac_ref, pick_ref, nwp_ref, sent_ref, out_ref, sem):
    fields, levels_in, count = nwp_ref.shape
    kept = lev_ref.shape[1]
    ids = lax.broadcasted_iota(jnp.int32, (levels_in, kept), 0)
    low, share = lev_ref[...], frac_ref[...]
    weight = jnp.where(ids == low, 1.0 - share, 0.0) + jnp.where(ids == low + 1, share, 0.0)
    parts = []
    for _ in range(3):
        part = weight.astype(BF16)
        weight = weight - part.astype(F32)
        parts.append(part)
    stacked = jnp.concatenate(parts, axis=1)
    rows = []
    for field in range(fields):
        mixed = lax.dot_general(
            stacked, nwp_ref[field], (((0,), (0,)), ((), ())), preferred_element_type=F32
        )
        rows.append((mixed[:kept] + mixed[kept : 2 * kept] + mixed[2 * kept :]).astype(BF16))
    levels = jnp.concatenate(rows, axis=0)
    half = LANES // 2
    width = 2 * LANES
    first = lane_ids((kept, LANES)) < half
    copies = []
    for block in range(pick_ref.shape[0] // 4):
        wanted = jnp.concatenate([pick_ref[4 * block + i : 4 * block + i + 1] for i in range(4)], axis=1)
        hit = one_hot(wanted, count)
        got = jnp.dot(levels, hit, preferred_element_type=F32)
        for h in range(2):
            east = got[:kept, h * LANES : (h + 1) * LANES]
            north = got[kept:, h * LANES : (h + 1) * LANES]
            out_ref[4 * block + 2 * h] = jnp.where(first, east, roll_lanes(north, half)).astype(BF16)
            out_ref[4 * block + 2 * h + 1] = jnp.where(
                first, roll_lanes(east, half), north
            ).astype(BF16)
        at = pl.ds(4 * block, 4)
        copies.append(pltpu.make_async_copy(out_ref.at[at], sent_ref.at[at], sem.at[block]))
        copies[-1].start()
    for copy in copies:
        copy.wait()


def horizontal_kernel(recv_ref, slot_ref, wt_ref, winds_ref, a_ref, b_ref, lev_ref):
    kept = recv_ref.shape[1]
    half = LANES // 2
    first = lane_ids((kept, LANES)) < half
    for pair in range(recv_ref.shape[0] // 2):
        one = recv_ref[2 * pair].astype(F32)
        two = recv_ref[2 * pair + 1].astype(F32)
        at = slice(pair * LANES, (pair + 1) * LANES)
        lev_ref[:kept, at] = jnp.where(first, one, roll_lanes(two, half)).astype(BF16)
        lev_ref[kept:, at] = jnp.where(first, roll_lanes(one, half), two).astype(BF16)
    rows = winds_ref.shape[0]
    lev = lev_ref[...]
    raw = [wt_ref[q] for q in range(4)]
    total = raw[0] + raw[1] + raw[2] + raw[3]
    norm = [w / total for w in raw]
    for y in range(0, rows, 2):
        winds = [None, None]
        for q in range(4):
            wanted = jnp.concatenate([slot_ref[q, y + h : y + h + 1] for h in range(2)], axis=1)
            got = jnp.dot(lev, one_hot(wanted, lev_ref.shape[1]), preferred_element_type=F32)
            for h in range(2):
                term = norm[q][y + h : y + h + 1] * got[:, h * LANES : (h + 1) * LANES]
                winds[h] = term if winds[h] is None else winds[h] + term
        winds_ref[y] = winds[0]
        winds_ref[y + 1] = winds[1]
    odd = lax.axis_index("rows") % 2 == 1
    for j in range(HALO):
        upper = winds_ref[j]
        lower = winds_ref[rows - HALO + j]
        a_ref[j] = jnp.where(odd, upper, lower).astype(BF16)
        b_ref[j] = jnp.where(odd, lower, upper).astype(BF16)


def swap(array, axis, first):
    peers = lax.axis_size(axis)
    start = 0 if first else 1
    pairs = []
    for i in range(start, peers - 1, 2):
        pairs += [(i, i + 1), (i + 1, i)]
    return lax.ppermute(array, axis, pairs)


def strip_select():
    lane = lane_ids((LANES, LANES))
    column = lax.broadcasted_iota(jnp.int32, (LANES, LANES), 0)
    chosen = []
    for i in range(STRIP_ROWS):
        at = lane - STRIP * i
        source = jnp.where(at < 3, at + 125, jnp.where(at < 5, at - 3, jnp.where(at < 7, at + 121, at - 7)))
        hit = (source == column) & (at >= 0) & (at < STRIP)
        chosen.append(jnp.where(hit, 1.0, 0.0).astype(BF16))
    return chosen


def whole_strip(mine, got_a, got_b, at, odd):
    from_left = jnp.where(odd, got_a, got_b)
    from_right = jnp.where(odd, got_b, got_a)
    return jnp.where(at < 3, from_left, jnp.where(at < 7, mine, from_right))


def side_strip_kernel(winds_ref, ra_ref, rb_ref, conc_ref, strip_ref):
    row_odd = lax.axis_index("rows") % 2 == 1
    rows = winds_ref.shape[0]
    chosen = strip_select()
    total = None
    for i in range(STRIP_ROWS):
        y = i - 2
        if 0 <= y < rows:
            line = winds_ref[y].astype(BF16)
        else:
            j = y + HALO if y < 0 else y - rows
            line = jnp.where(row_odd == (y < 0), ra_ref[j], rb_ref[j])
        term = jnp.dot(line, chosen[i], preferred_element_type=F32)
        total = term if total is None else total + term
    before = conc_ref.shape[0]
    strip_ref[:before] = conc_ref[...]
    strip_ref[before:] = total.astype(BF16)


def conc_edge_kernel(conc_ref, mask_ref, a_ref, b_ref):
    odd = lax.axis_index("rows") % 2 == 1
    bins = a_ref.shape[2] // 2
    pairs = a_ref.shape[1] - 1
    rows = mask_ref.shape[0]
    stride = 2 * pairs * rows

    def pair(p, carry):
        for j in range(HALO):
            upper, lower = (
                jnp.concatenate(
                    [conc_ref[pl.ds((2 * p + h) * rows + y, bins, stride=stride), :] for h in range(2)]
                )
                for y in (j, rows - HALO + j)
            )
            a_ref[j, p] = jnp.where(odd, upper, lower).astype(BF16)
            b_ref[j, p] = jnp.where(odd, lower, upper).astype(BF16)
        return carry

    lax.fori_loop(0, pairs, pair, 0, unroll=4)
    mask = mask_ref[...].astype(F32)
    for j in range(HALO):
        upper = jnp.broadcast_to(mask[j : j + 1], (2 * bins, LANES))
        lower = jnp.broadcast_to(mask[rows - HALO + j : rows - HALO + j + 1], (2 * bins, LANES))
        a_ref[j, pairs] = jnp.where(odd, upper, lower).astype(BF16)
        b_ref[j, pairs] = jnp.where(odd, lower, upper).astype(BF16)


def conc_strip_kernel(conc_ref, mask_ref, ra_ref, rb_ref, strip_ref, line_ref):
    row_odd = lax.axis_index("rows") % 2 == 1
    pairs = ra_ref.shape[1] - 1
    two = ra_ref.shape[2]
    bins = two // 2
    rows = mask_ref.shape[0]
    stride = 2 * pairs * rows
    mask = mask_ref[...].astype(F32)
    chosen = strip_select()
    total = None
    for i in range(STRIP_ROWS):
        y = i - 2
        for p in range(pairs + 1):
            if not 0 <= y < rows:
                j = y + HALO if y < 0 else y - rows
                both = jnp.where(row_odd == (y < 0), ra_ref[j, p], rb_ref[j, p])
            elif p < pairs:
                both = jnp.concatenate(
                    [conc_ref[pl.ds((2 * p + h) * rows + y, bins, stride=stride), :] for h in range(2)]
                ).astype(BF16)
            else:
                both = jnp.broadcast_to(mask[y : y + 1], (two, LANES)).astype(BF16)
            line_ref[i % 2, p * two : (p + 1) * two] = both
        term = jnp.dot(line_ref[i % 2], chosen[i], preferred_element_type=F32)
        total = term if total is None else total + term
    strip_ref[...] = total.astype(BF16)


def coefficients(face_w, face_e, face_s, face_n):
    return (
        (1.0 - 4.0 * KAPPA)
        - (jnp.maximum(face_e, 0.0) - jnp.minimum(face_w, 0.0))
        - (jnp.maximum(face_n, 0.0) - jnp.minimum(face_s, 0.0)),
        KAPPA + jnp.maximum(face_w, 0.0),
        KAPPA - jnp.minimum(face_e, 0.0),
        KAPPA + jnp.maximum(face_s, 0.0),
        KAPPA - jnp.minimum(face_n, 0.0),
    )


def halo_at(y, rows):
    return y + HALO if y < 0 else y - rows


def settle_tile(settle_ref, tile):
    sublanes = lax.broadcasted_iota(jnp.int32, tile, 0)
    settle = jnp.zeros(tile, F32)
    for b in range(tile[0]):
        settle = jnp.where(sublanes == b, settle_ref[b], settle)
    return settle


def first_step_kernel(
    conc_ref, settle_ref, ra_ref, rb_ref, winds_ref, wra_ref, wrb_ref,
    coef_ref, part_ref, deposit_ref, fall_ref,
):
    row, last_row = lax.axis_index("rows"), lax.axis_size("rows") - 1
    row_odd = row % 2 == 1
    levels = coef_ref.shape[1]
    bins = ra_ref.shape[2] // 2
    rows = winds_ref.shape[0]
    tile = (bins, LANES)
    stride = levels * rows

    def wind_row(y):
        if 0 <= y < rows:
            return winds_ref[y]
        j = halo_at(y, rows)
        return jnp.where(row_odd == (y < 0), wra_ref[j].astype(F32), wrb_ref[j].astype(F32))

    lanes = lane_ids((levels, LANES))
    at_west, at_east = lanes == 0, lanes == LANES - 1
    for y in range(-2, rows + 2):
        u = wind_row(y)[:levels]
        north_s, north, north_n = (wind_row(y + d)[levels:] for d in (-1, 0, 1))
        face_w = jnp.where(at_west, 0.0, 0.5 * (roll_lanes(u, 1) + u))
        face_e = jnp.where(at_east, 0.0, 0.5 * (u + roll_lanes(u, -1)))
        found = coefficients(face_w, face_e, 0.5 * (north_s + north), 0.5 * (north + north_n))
        if not 0 <= y < rows:
            valid = row > 0 if y < 0 else row < last_row
            found = [jnp.where(valid, c, 0.0) for c in found]
        found = [
            found[0], jnp.where(at_west, 0.0, found[1]), jnp.where(at_east, 0.0, found[2]), *found[3:]
        ]
        for i in range(5):
            coef_ref[5 * (y + 2) + i] = found[i]

    settle = settle_tile(settle_ref, tile)
    fall_ref[...] = jnp.zeros(fall_ref.shape, F32)
    unroll = 16

    def some_levels(trip, carry):
        ks = [trip * unroll + u for u in range(unroll)]

        def starts_of(y):
            if 0 <= y < rows:
                return [conc_ref[pl.ds(k * rows + y, bins, stride=stride), :] for k in ks]
            j = halo_at(y, rows)
            result = []
            for p in range(unroll // 2):
                at = trip * (unroll // 2) + p
                both = jnp.where(row_odd == (y < 0), ra_ref[j, at].astype(F32), rb_ref[j, at].astype(F32))
                result += [both[:bins], both[bins:]]
            return result

        below, here = starts_of(-3), starts_of(-2)
        for y in range(-2, rows + 2):
            above = starts_of(y + 1)
            fall = fall_ref[y + 2]
            for u, k in enumerate(ks):
                c = [coef_ref[5 * (y + 2) + i, pl.ds(k, bins, stride=0), :] for i in range(5)]
                a = here[u]
                part_ref[y + 2, pl.ds(k * bins, bins), :] = (
                    (c[0] - settle) * a
                    + (c[1] * roll_lanes(a, 1) + c[2] * roll_lanes(a, -1))
                    + (c[3] * below[u] + c[4] * above[u])
                    + fall
                )
                fall = settle * a
            fall_ref[y + 2] = fall
            below, here = here, above
        return carry

    lax.fori_loop(0, levels // unroll, some_levels, 0)
    for y in range(rows):
        deposit_ref[y] = fall_ref[y + 2]


def transport_kernel(
    part_ref, coef_ref, fallen_ref, mask_ref, settle_ref, profile_ref,
    ra_ref, rb_ref, own_ref, xa_ref, xb_ref,
    out_ref, deposit_ref,
    centre_ref, strip_coef_ref, bound_ref, source_ref, fall_ref,
):
    row, col = lax.axis_index("rows"), lax.axis_index("cols")
    last_row, last_col = lax.axis_size("rows") - 1, lax.axis_size("cols") - 1
    row_odd, col_odd = row % 2 == 1, col % 2 == 1
    levels = coef_ref.shape[1]
    two = ra_ref.shape[2]
    bins = two // 2
    rows = mask_ref.shape[0]
    tile = (bins, LANES)
    stride = levels * rows

    def strip_at(start, size):
        at = pl.ds(start, size)
        return whole_strip(
            own_ref[at, :].astype(F32), xa_ref[at, :].astype(F32), xb_ref[at, :].astype(F32),
            lane_ids((size, LANES)) % STRIP, col_odd,
        )

    lanes = lane_ids((levels, LANES))
    at = lanes % STRIP
    winds_at = (levels + 2) * bins
    strip_u, strip_v = strip_at(winds_at, levels), strip_at(winds_at + levels, levels)
    inside = (
        ((at >= 3) | (col > 0))
        & ((at < 7) | (col < last_col))
        & ((lanes >= 2 * STRIP) | (row > 0))
        & ((lanes < (2 + rows) * STRIP) | (row < last_row))
    )
    face_w = 0.5 * (roll_lanes(strip_u, 1) + strip_u)
    face_e = 0.5 * (strip_u + roll_lanes(strip_u, -1))
    found = coefficients(
        face_w, face_e,
        0.5 * (roll_lanes(strip_v, STRIP) + strip_v),
        0.5 * (strip_v + roll_lanes(strip_v, -STRIP)),
    )
    for i in range(5):
        strip_coef_ref[i] = jnp.where(inside, found[i], 0.0)
    sides = jnp.where(at == 3, jnp.minimum(face_w, 0.0), jnp.where(at == 6, -jnp.maximum(face_e, 0.0), 0.0))
    sides = jnp.where(inside, sides, 0.0)
    strip_coef_ref[5] = sides
    for y in range(-1, rows + 1):
        base = STRIP * (y + 2)
        west = roll_lanes(sides, -(base + 3))
        east = roll_lanes(sides, LANES - 1 - (base + 6))
        more = jnp.where(lanes == 0, west, jnp.where(lanes == LANES - 1, east, 0.0))
        centre_ref[y + 1] = coef_ref[5 * (y + 2)] + more

    settle = settle_tile(settle_ref, tile)

    tile_lanes = lane_ids(tile)
    tile_at = tile_lanes % STRIP
    spare = STRIP * STRIP_ROWS
    mask_strip = strip_at(levels * bins, two)[:bins]
    fall_before = [jnp.zeros(tile, F32)] * (STEPS - 1)
    flows = [[] for _ in range(STEPS)]
    edges = None
    for k in range(levels):
        if k % 2 == 0:
            edges = strip_at(k * bins, two)
        edge = edges[:bins] if k % 2 == 0 else edges[bins:]
        prof = jnp.broadcast_to(profile_ref[:, k : k + 1], tile)
        parts = []
        rest = prof
        for _ in range(3):
            part = rest.astype(BF16).astype(F32)
            rest = rest - part
            parts.append(part)
        emitted = prof * mask_strip
        c = [jnp.broadcast_to(strip_coef_ref[i, k : k + 1, :], tile) for i in range(6)]
        for step in range(STEPS):
            from_w = c[1] * roll_lanes(edge, 1)
            from_e = c[2] * roll_lanes(edge, -1)
            flow = jnp.where(tile_at == 3, from_w, jnp.where(tile_at == 6, from_e, 0.0))
            if step == 0:
                flow = flow + c[5] * edge
            for i, part in enumerate(parts):
                flow = jnp.where(tile_lanes == spare + i, part, flow)
            flow = jnp.where(tile_lanes >= spare + 3, 0.0, flow)
            flows[step].append(flow)
            if k % 2:
                bound_ref[step, (k - 1) * bins : (k + 1) * bins] = jnp.concatenate(flows[step][-2:]).astype(BF16)
            if step < STEPS - 1:
                fall = settle * edge
                edge = (
                    (c[0] * edge - fall)
                    + (from_w + from_e)
                    + (c[3] * roll_lanes(edge, STRIP) + c[4] * roll_lanes(edge, -STRIP))
                    + (fall_before[step] + emitted)
                )
                fall_before[step] = fall

    lane_of = lax.broadcasted_iota(jnp.int32, (LANES, LANES), 0)
    x_of = lane_ids((LANES, LANES))
    mask = mask_ref[...].astype(F32)
    last_pair = ra_ref.shape[1] - 1
    spread = []
    for y in range(-2, rows + 2):
        base = STRIP * (y + 2)
        hit = ((x_of == 0) & (lane_of == base + 3)) | ((x_of == LANES - 1) & (lane_of == base + 6))
        if 0 <= y < rows:
            line = mask[y : y + 1]
        else:
            j = halo_at(y, rows)
            line = jnp.where(
                row_odd == (y < 0), ra_ref[j, last_pair].astype(F32), rb_ref[j, last_pair].astype(F32)
            )[:1]
        emits = (lane_of >= spare) & (lane_of < spare + 3)
        table = jnp.where(hit, 1.0, jnp.where(emits, line, 0.0)).astype(BF16)
        spread.append(table)
    slot = 0
    slots = {}
    for step in range(STEPS):
        both = bound_ref[step]
        reach = STEPS - 1 - step
        for y in range(-reach, rows + reach, 2):
            pair = jnp.concatenate([spread[y + 2], spread[y + 3]], axis=1)
            got = jnp.dot(both, pair, preferred_element_type=F32)
            for side in range(2):
                slots[step, y + side] = slot
                source_ref[slot] = got[:, side * LANES : (side + 1) * LANES]
                slot += 1

    fall_ref[...] = jnp.zeros(fall_ref.shape, F32)
    unroll = 16
    skipped = slots[1, -1]

    def some_levels(trip, carry):
        ks = [trip * unroll + u for u in range(unroll)]
        coefs = [{} for _ in ks]
        states = [[{} for _ in range(STEPS + 1)] for _ in ks]
        for front in range(-2, rows + 4):
            for step in range(STEPS):
                y = front - step
                reach = STEPS - 1 - step
                if not -reach <= y < rows + reach:
                    continue
                index = slots[step, y]
                if step == 0:
                    for u, k in enumerate(ks):
                        at_k = pl.ds(k * bins, bins)
                        states[u][1][y] = part_ref[y + 2, at_k, :] + source_ref[index, at_k, :]
                    continue
                fall = fall_ref[index - skipped]
                for u, k in enumerate(ks):
                    if step == 1:
                        coefs[u][y] = [centre_ref[y + 1, pl.ds(k, bins, stride=0), :] - settle] + [
                            coef_ref[5 * (y + 2) + i, pl.ds(k, bins, stride=0), :] for i in range(1, 5)
                        ]
                    state = states[u][step]
                    c = coefs[u][y]
                    a = state[y]
                    source = source_ref[index, pl.ds(k * bins, bins), :] + fall
                    fall = settle * a
                    fresh = (
                        c[0] * a
                        + (c[1] * roll_lanes(a, 1) + c[2] * roll_lanes(a, -1))
                        + (c[3] * state[y - 1] + c[4] * state[y + 1])
                        + source
                    )
                    if step < STEPS - 1:
                        states[u][step + 1][y] = fresh
                    else:
                        out_ref[pl.ds(k * rows + y, bins, stride=stride), :] = fresh
                fall_ref[index - skipped] = fall
        return carry

    lax.fori_loop(0, levels // unroll, some_levels, 0)
    for y in range(rows):
        deposit_ref[pl.ds(y, bins, stride=rows), :] = (
            fallen_ref[y] + fall_ref[slots[1, y] - skipped] + fall_ref[slots[2, y] - skipped]
        )


def per_device(conc, nwp, lev_lo, frac, pick, corner_slot, corner_wt, settle, source_mask, profile):
    bins, levels, rows, cols = conc.shape
    peers = pick.shape[2]
    shape = jax.ShapeDtypeStruct
    flat = conc.reshape(bins * levels * rows, cols)

    sent = call(
        select_kernel,
        shape((peers, levels, LANES), BF16),
        (lev_lo.reshape(1, -1), frac.reshape(1, -1), pick.reshape(peers, -1), nwp),
        scratch=(
            pltpu.VMEM((peers, levels, LANES), BF16),
            pltpu.SemaphoreType.DMA((peers // 4,)),
        ),
        out_spaces=(pltpu.HBM,),
        flops=2 * 2 * levels * 2048 * 2048,
    )

    flat, sent = lax.optimization_barrier((flat, sent))
    received = lax.all_to_all(sent, "rows", split_axis=0, concat_axis=0, tiled=True)

    pairs = levels // 2 + 1
    edge_rows = shape((HALO, pairs, 2 * bins, cols), BF16)
    ca, cb = call(conc_edge_kernel, (edge_rows, edge_rows), (flat, source_mask), moved=0)
    ra, rb = swap(ca, "rows", True), swap(cb, "rows", False)

    wind_rows = shape((HALO, 2 * levels, cols), BF16)
    winds, wa, wb = call(
        horizontal_kernel,
        (shape((rows, 2 * levels, cols), F32), wind_rows, wind_rows),
        (received, corner_slot, corner_wt),
        scratch=(pltpu.VMEM((2 * levels, peers * LANES // 2), BF16),),
        flops=HIDES,
        limit=20,
    )
    wra, wrb = swap(wa, "rows", True), swap(wb, "rows", False)

    ra, rb, wa = lax.optimization_barrier((ra, rb, wa))
    strips = shape((pairs * 2 * bins, LANES), BF16)
    conc_strip = call(
        conc_strip_kernel, strips, (flat, source_mask, ra, rb),
        scratch=(pltpu.VMEM((2, pairs * 2 * bins, LANES), BF16),),
        moved=0,
    )
    own = call(
        side_strip_kernel,
        shape((pairs * 2 * bins + 2 * levels, LANES), BF16),
        (winds, wra, wrb, conc_strip),
        flops=HIDES,
    )
    xa, xb = swap(own, "cols", True), swap(own, "cols", False)

    tile = (bins, LANES)
    part, coef, fallen = (
        shape((rows + 4, levels * bins, LANES), F32),
        shape((5 * (rows + 4), levels, LANES), F32),
        shape((rows,) + tile, F32),
    )
    coef, part, fallen = call(
        first_step_kernel,
        (coef, part, fallen),
        (flat, settle, ra, rb, winds, wra, wrb),
        scratch=(pltpu.VMEM((rows + 4,) + tile, F32),),
        smem=(1,),
        moved=0,
    )
    updates = sum(rows + 2 * (STEPS - 1 - s) for s in range(STEPS))
    final, deposit = call(
        transport_kernel,
        (shape(flat.shape, F32), shape((bins * rows, cols), F32)),
        (part, coef, fallen, source_mask, settle, profile, ra, rb, own, xa, xb),
        scratch=(
            pltpu.VMEM((rows + 2, levels, LANES), F32),
            pltpu.VMEM((6, levels, LANES), F32),
            pltpu.VMEM((STEPS, levels * bins, LANES), BF16),
            pltpu.VMEM((updates, levels * bins, LANES), F32),
            pltpu.VMEM((updates - rows - 4,) + tile, F32),
        ),
        smem=(4,),
        flops=16 * updates * levels * bins * LANES,
        limit=24,
    )
    return final.reshape(conc.shape), deposit.reshape(bins, rows, cols)


def solution(mesh):
    placed = (
        P(None, None, "rows", "cols"),
        P(None, None, "rows"),
        P(),
        P(),
        P("rows", "cols", None, None),
        P(None, "rows", "cols"),
        P(None, "rows", "cols"),
        P(),
        P("rows", "cols"),
        P(),
    )
    return jax.shard_map(
        per_device,
        mesh=mesh,
        in_specs=placed,
        out_specs=(P(None, None, "rows", "cols"), P(None, "rows", "cols")),
        check_vma=False,
    )
```

```python
import functools

import jax
import jax.numpy as jnp
from jax import lax
from jax.experimental import pallas as pl
from jax.experimental.pallas import tpu as pltpu
from jax.sharding import PartitionSpec as P

STEPS = 3
KAPPA = 0.05
HALO = STEPS
LANES = 128
STRIP = 10
STRIP_ROWS = 12
F32 = jnp.float32
BF16 = jnp.bfloat16
SPLIT = 64
MIB = 1024 * 1024
HIDES = 50_000_000_000


def lane_ids(shape):
    return lax.broadcasted_iota(jnp.int32, shape, len(shape) - 1)


def roll_lanes(x, shift):
    return pltpu.roll(x, shift % LANES, x.ndim - 1)


def call(kernel, out_shape, args, scratch=(), flops=0, smem=(), limit=16, moved=None, out_spaces=None):
    if moved is None:
        moved = sum(a.size * a.dtype.itemsize for a in args) + sum(
            s.size * s.dtype.itemsize for s in jax.tree.leaves(out_shape)
        )
    leaves, tree = jax.tree.flatten(out_shape)
    spaces = out_spaces or (pltpu.VMEM,) * len(leaves)
    return pl.pallas_call(
        kernel,
        out_shape=out_shape,
        in_specs=[
            pl.BlockSpec(memory_space=pltpu.SMEM if i in smem else pltpu.VMEM)
            for i in range(len(args))
        ],
        out_specs=jax.tree.unflatten(tree, [pl.BlockSpec(memory_space=m) for m in spaces]),
        scratch_shapes=list(scratch),
        compiler_params=pltpu.CompilerParams(vmem_limit_bytes=limit * MIB),
        cost_estimate=pl.CostEstimate(flops=flops, bytes_accessed=moved, transcendentals=0),
    )(*args)


def one_hot(wanted, count):
    width = wanted.shape[1]
    group = wanted // SPLIT
    place = lax.broadcasted_iota(jnp.int32, (SPLIT, width), 0)
    unit = jnp.where(place == wanted - group * SPLIT, 1.0, 0.0).astype(BF16)
    none = jnp.zeros((SPLIT, width), BF16)
    group = jnp.broadcast_to(group.astype(F32), (SPLIT, width)).astype(BF16)
    return jnp.concatenate([jnp.where(group == g, unit, none) for g in range(count // SPLIT)], axis=0)


def select_kernel(lev_ref, frac_ref, pick_ref, nwp_ref, sent_ref, out_ref, sem):
    fields, levels_in, count = nwp_ref.shape
    kept = lev_ref.shape[1]
    ids = lax.broadcasted_iota(jnp.int32, (levels_in, kept), 0)
    low, share = lev_ref[...], frac_ref[...]
    weight = jnp.where(ids == low, 1.0 - share, 0.0) + jnp.where(ids == low + 1, share, 0.0)
    parts = []
    for _ in range(3):
        part = weight.astype(BF16)
        weight = weight - part.astype(F32)
        parts.append(part)
    stacked = jnp.concatenate(parts, axis=1)
    rows = []
    for field in range(fields):
        mixed = lax.dot_general(
            stacked, nwp_ref[field], (((0,), (0,)), ((), ())), preferred_element_type=F32
        )
        rows.append((mixed[:kept] + mixed[kept : 2 * kept] + mixed[2 * kept :]).astype(BF16))
    levels = jnp.concatenate(rows, axis=0)
    half = LANES // 2
    width = 2 * LANES
    first = lane_ids((kept, LANES)) < half
    copies = []
    for block in range(pick_ref.shape[0] // 4):
        wanted = jnp.concatenate([pick_ref[4 * block + i : 4 * block + i + 1] for i in range(4)], axis=1)
        hit = one_hot(wanted, count)
        got = jnp.dot(levels, hit, preferred_element_type=F32)
        for h in range(2):
            east = got[:kept, h * LANES : (h + 1) * LANES]
            north = got[kept:, h * LANES : (h + 1) * LANES]
            out_ref[4 * block + 2 * h] = jnp.where(first, east, roll_lanes(north, half)).astype(BF16)
            out_ref[4 * block + 2 * h + 1] = jnp.where(
                first, roll_lanes(east, half), north
            ).astype(BF16)
        at = pl.ds(4 * block, 4)
        copies.append(pltpu.make_async_copy(out_ref.at[at], sent_ref.at[at], sem.at[block]))
        copies[-1].start()
    for copy in copies:
        copy.wait()


def horizontal_kernel(recv_ref, slot_ref, wt_ref, winds_ref, a_ref, b_ref, lev_ref):
    kept = recv_ref.shape[1]
    half = LANES // 2
    for pair in range(recv_ref.shape[0] // 2):
        one, two = recv_ref[2 * pair], recv_ref[2 * pair + 1]
        at = slice(pair * LANES, (pair + 1) * LANES)
        lev_ref[:kept, at] = jnp.concatenate([one[:, :half], two[:, :half]], axis=1)
        lev_ref[kept:, at] = jnp.concatenate([one[:, half:], two[:, half:]], axis=1)
    rows = winds_ref.shape[0]
    lev = lev_ref[...]
    raw = [wt_ref[q] for q in range(4)]
    total = raw[0] + raw[1] + raw[2] + raw[3]
    norm = [w / total for w in raw]
    for y in range(0, rows, 2):
        winds = [None, None]
        for q in range(4):
            wanted = jnp.concatenate([slot_ref[q, y + h : y + h + 1] for h in range(2)], axis=1)
            got = jnp.dot(lev, one_hot(wanted, lev_ref.shape[1]), preferred_element_type=F32)
            for h in range(2):
                term = norm[q][y + h : y + h + 1] * got[:, h * LANES : (h + 1) * LANES]
                winds[h] = term if winds[h] is None else winds[h] + term
        winds_ref[y] = winds[0]
        winds_ref[y + 1] = winds[1]
    odd = lax.axis_index("rows") % 2 == 1
    for j in range(HALO):
        upper = winds_ref[j]
        lower = winds_ref[rows - HALO + j]
        a_ref[j] = jnp.where(odd, upper, lower).astype(BF16)
        b_ref[j] = jnp.where(odd, lower, upper).astype(BF16)


def swap(array, axis, first):
    peers = lax.axis_size(axis)
    start = 0 if first else 1
    pairs = []
    for i in range(start, peers - 1, 2):
        pairs += [(i, i + 1), (i + 1, i)]
    return lax.ppermute(array, axis, pairs)


def strip_select():
    lane = lane_ids((LANES, LANES))
    column = lax.broadcasted_iota(jnp.int32, (LANES, LANES), 0)
    chosen = []
    for i in range(STRIP_ROWS):
        at = lane - STRIP * i
        source = jnp.where(at < 3, at + 125, jnp.where(at < 5, at - 3, jnp.where(at < 7, at + 121, at - 7)))
        hit = (source == column) & (at >= 0) & (at < STRIP)
        chosen.append(jnp.where(hit, 1.0, 0.0).astype(BF16))
    return chosen


def whole_strip(mine, got_a, got_b, at, odd):
    from_left = jnp.where(odd, got_a, got_b)
    from_right = jnp.where(odd, got_b, got_a)
    return jnp.where(at < 3, from_left, jnp.where(at < 7, mine, from_right))


def side_strip_kernel(winds_ref, ra_ref, rb_ref, conc_ref, strip_ref):
    row_odd = lax.axis_index("rows") % 2 == 1
    rows = winds_ref.shape[0]
    chosen = strip_select()
    total = None
    for i in range(STRIP_ROWS):
        y = i - 2
        if 0 <= y < rows:
            line = winds_ref[y].astype(BF16)
        else:
            j = y + HALO if y < 0 else y - rows
            line = jnp.where(row_odd == (y < 0), ra_ref[j], rb_ref[j])
        term = jnp.dot(line, chosen[i], preferred_element_type=F32)
        total = term if total is None else total + term
    before = conc_ref.shape[0]
    strip_ref[:before] = conc_ref[...]
    strip_ref[before:] = total.astype(BF16)


def conc_edge_kernel(conc_ref, mask_ref, a_ref, b_ref):
    odd = lax.axis_index("rows") % 2 == 1
    bins = a_ref.shape[2] // 2
    pairs = a_ref.shape[1] - 1
    rows = mask_ref.shape[0]
    stride = 2 * pairs * rows

    def pair(p, carry):
        for j in range(HALO):
            upper, lower = (
                jnp.concatenate(
                    [conc_ref[pl.ds((2 * p + h) * rows + y, bins, stride=stride), :] for h in range(2)]
                )
                for y in (j, rows - HALO + j)
            )
            a_ref[j, p] = jnp.where(odd, upper, lower).astype(BF16)
            b_ref[j, p] = jnp.where(odd, lower, upper).astype(BF16)
        return carry

    lax.fori_loop(0, pairs, pair, 0, unroll=4)
    mask = mask_ref[...].astype(F32)
    for j in range(HALO):
        upper = jnp.broadcast_to(mask[j : j + 1], (2 * bins, LANES))
        lower = jnp.broadcast_to(mask[rows - HALO + j : rows - HALO + j + 1], (2 * bins, LANES))
        a_ref[j, pairs] = jnp.where(odd, upper, lower).astype(BF16)
        b_ref[j, pairs] = jnp.where(odd, lower, upper).astype(BF16)


def conc_strip_kernel(conc_ref, mask_ref, ra_ref, rb_ref, strip_ref, line_ref):
    row_odd = lax.axis_index("rows") % 2 == 1
    pairs = ra_ref.shape[1] - 1
    two = ra_ref.shape[2]
    bins = two // 2
    rows = mask_ref.shape[0]
    stride = 2 * pairs * rows
    mask = mask_ref[...].astype(F32)
    chosen = strip_select()
    total = None
    for i in range(STRIP_ROWS):
        y = i - 2
        for p in range(pairs + 1):
            if not 0 <= y < rows:
                j = y + HALO if y < 0 else y - rows
                both = jnp.where(row_odd == (y < 0), ra_ref[j, p], rb_ref[j, p])
            elif p < pairs:
                both = jnp.concatenate(
                    [conc_ref[pl.ds((2 * p + h) * rows + y, bins, stride=stride), :] for h in range(2)]
                ).astype(BF16)
            else:
                both = jnp.broadcast_to(mask[y : y + 1], (two, LANES)).astype(BF16)
            line_ref[i % 2, p * two : (p + 1) * two] = both
        term = jnp.dot(line_ref[i % 2], chosen[i], preferred_element_type=F32)
        total = term if total is None else total + term
    strip_ref[...] = total.astype(BF16)


def coefficients(face_w, face_e, face_s, face_n):
    return (
        (1.0 - 4.0 * KAPPA)
        - (jnp.maximum(face_e, 0.0) - jnp.minimum(face_w, 0.0))
        - (jnp.maximum(face_n, 0.0) - jnp.minimum(face_s, 0.0)),
        KAPPA + jnp.maximum(face_w, 0.0),
        KAPPA - jnp.minimum(face_e, 0.0),
        KAPPA + jnp.maximum(face_s, 0.0),
        KAPPA - jnp.minimum(face_n, 0.0),
    )


def halo_at(y, rows):
    return y + HALO if y < 0 else y - rows


def settle_tile(settle_ref, tile):
    sublanes = lax.broadcasted_iota(jnp.int32, tile, 0)
    settle = jnp.zeros(tile, F32)
    for b in range(tile[0]):
        settle = jnp.where(sublanes == b, settle_ref[b], settle)
    return settle


def first_step_kernel(
    conc_ref, settle_ref, ra_ref, rb_ref, winds_ref, wra_ref, wrb_ref,
    coef_ref, part_ref, deposit_ref, fall_ref,
):
    row, last_row = lax.axis_index("rows"), lax.axis_size("rows") - 1
    row_odd = row % 2 == 1
    levels = coef_ref.shape[1]
    bins = ra_ref.shape[2] // 2
    rows = winds_ref.shape[0]
    tile = (bins, LANES)
    stride = levels * rows

    def wind_row(y):
        if 0 <= y < rows:
            return winds_ref[y]
        j = halo_at(y, rows)
        return jnp.where(row_odd == (y < 0), wra_ref[j].astype(F32), wrb_ref[j].astype(F32))

    lanes = lane_ids((levels, LANES))
    at_west, at_east = lanes == 0, lanes == LANES - 1
    for y in range(-2, rows + 2):
        u = wind_row(y)[:levels]
        north_s, north, north_n = (wind_row(y + d)[levels:] for d in (-1, 0, 1))
        face_w = jnp.where(at_west, 0.0, 0.5 * (roll_lanes(u, 1) + u))
        face_e = jnp.where(at_east, 0.0, 0.5 * (u + roll_lanes(u, -1)))
        found = coefficients(face_w, face_e, 0.5 * (north_s + north), 0.5 * (north + north_n))
        if not 0 <= y < rows:
            valid = row > 0 if y < 0 else row < last_row
            found = [jnp.where(valid, c, 0.0) for c in found]
        found = [
            found[0], jnp.where(at_west, 0.0, found[1]), jnp.where(at_east, 0.0, found[2]), *found[3:]
        ]
        for i in range(5):
            coef_ref[5 * (y + 2) + i] = found[i]

    settle = settle_tile(settle_ref, tile)
    fall_ref[...] = jnp.zeros(fall_ref.shape, F32)
    unroll = 16

    def some_levels(trip, carry):
        ks = [trip * unroll + u for u in range(unroll)]

        def starts_of(y):
            if 0 <= y < rows:
                return [conc_ref[pl.ds(k * rows + y, bins, stride=stride), :] for k in ks]
            j = halo_at(y, rows)
            result = []
            for p in range(unroll // 2):
                at = trip * (unroll // 2) + p
                both = jnp.where(row_odd == (y < 0), ra_ref[j, at].astype(F32), rb_ref[j, at].astype(F32))
                result += [both[:bins], both[bins:]]
            return result

        below, here = starts_of(-3), starts_of(-2)
        for y in range(-2, rows + 2):
            above = starts_of(y + 1)
            fall = fall_ref[y + 2]
            for u, k in enumerate(ks):
                c = [coef_ref[5 * (y + 2) + i, pl.ds(k, bins, stride=0), :] for i in range(5)]
                a = here[u]
                part_ref[y + 2, pl.ds(k * bins, bins), :] = (
                    (c[0] - settle) * a
                    + (c[1] * roll_lanes(a, 1) + c[2] * roll_lanes(a, -1))
                    + (c[3] * below[u] + c[4] * above[u])
                    + fall
                )
                fall = settle * a
            fall_ref[y + 2] = fall
            below, here = here, above
        return carry

    lax.fori_loop(0, levels // unroll, some_levels, 0)
    for y in range(rows):
        deposit_ref[y] = fall_ref[y + 2]


def transport_kernel(
    part_ref, coef_ref, fallen_ref, mask_ref, settle_ref, profile_ref,
    ra_ref, rb_ref, own_ref, xa_ref, xb_ref,
    out_ref, deposit_ref,
    centre_ref, strip_coef_ref, bound_ref, source_ref, fall_ref,
):
    row, col = lax.axis_index("rows"), lax.axis_index("cols")
    last_row, last_col = lax.axis_size("rows") - 1, lax.axis_size("cols") - 1
    row_odd, col_odd = row % 2 == 1, col % 2 == 1
    levels = coef_ref.shape[1]
    two = ra_ref.shape[2]
    bins = two // 2
    rows = mask_ref.shape[0]
    tile = (bins, LANES)
    stride = levels * rows

    def strip_at(start, size):
        at = pl.ds(start, size)
        return whole_strip(
            own_ref[at, :].astype(F32), xa_ref[at, :].astype(F32), xb_ref[at, :].astype(F32),
            lane_ids((size, LANES)) % STRIP, col_odd,
        )

    lanes = lane_ids((levels, LANES))
    at = lanes % STRIP
    winds_at = (levels + 2) * bins
    strip_u, strip_v = strip_at(winds_at, levels), strip_at(winds_at + levels, levels)
    inside = (
        ((at >= 3) | (col > 0))
        & ((at < 7) | (col < last_col))
        & ((lanes >= 2 * STRIP) | (row > 0))
        & ((lanes < (2 + rows) * STRIP) | (row < last_row))
    )
    face_w = 0.5 * (roll_lanes(strip_u, 1) + strip_u)
    face_e = 0.5 * (strip_u + roll_lanes(strip_u, -1))
    found = coefficients(
        face_w, face_e,
        0.5 * (roll_lanes(strip_v, STRIP) + strip_v),
        0.5 * (strip_v + roll_lanes(strip_v, -STRIP)),
    )
    for i in range(5):
        strip_coef_ref[i] = jnp.where(inside, found[i], 0.0)
    sides = jnp.where(at == 3, jnp.minimum(face_w, 0.0), jnp.where(at == 6, -jnp.maximum(face_e, 0.0), 0.0))
    sides = jnp.where(inside, sides, 0.0)
    strip_coef_ref[5] = sides
    for y in range(-1, rows + 1):
        base = STRIP * (y + 2)
        west = roll_lanes(sides, -(base + 3))
        east = roll_lanes(sides, LANES - 1 - (base + 6))
        more = jnp.where(lanes == 0, west, jnp.where(lanes == LANES - 1, east, 0.0))
        centre_ref[y + 1] = coef_ref[5 * (y + 2)] + more

    settle = settle_tile(settle_ref, tile)

    tile_lanes = lane_ids(tile)
    tile_at = tile_lanes % STRIP
    spare = STRIP * STRIP_ROWS
    mask_strip = strip_at(levels * bins, two)[:bins]
    fall_before = [jnp.zeros(tile, F32)] * (STEPS - 1)
    flows = [[] for _ in range(STEPS)]
    edges = None
    for k in range(levels):
        if k % 2 == 0:
            edges = strip_at(k * bins, two)
        edge = edges[:bins] if k % 2 == 0 else edges[bins:]
        prof = jnp.broadcast_to(profile_ref[:, k : k + 1], tile)
        parts = []
        rest = prof
        for _ in range(3):
            part = rest.astype(BF16).astype(F32)
            rest = rest - part
            parts.append(part)
        emitted = prof * mask_strip
        c = [jnp.broadcast_to(strip_coef_ref[i, k : k + 1, :], tile) for i in range(6)]
        for step in range(STEPS):
            from_w = c[1] * roll_lanes(edge, 1)
            from_e = c[2] * roll_lanes(edge, -1)
            flow = jnp.where(tile_at == 3, from_w, jnp.where(tile_at == 6, from_e, 0.0))
            if step == 0:
                flow = flow + c[5] * edge
            for i, part in enumerate(parts):
                flow = jnp.where(tile_lanes == spare + i, part, flow)
            flow = jnp.where(tile_lanes >= spare + 3, 0.0, flow)
            flows[step].append(flow)
            if k % 2:
                bound_ref[step, (k - 1) * bins : (k + 1) * bins] = jnp.concatenate(flows[step][-2:]).astype(BF16)
            if step < STEPS - 1:
                fall = settle * edge
                edge = (
                    (c[0] * edge - fall)
                    + (from_w + from_e)
                    + (c[3] * roll_lanes(edge, STRIP) + c[4] * roll_lanes(edge, -STRIP))
                    + (fall_before[step] + emitted)
                )
                fall_before[step] = fall

    lane_of = lax.broadcasted_iota(jnp.int32, (LANES, LANES), 0)
    x_of = lane_ids((LANES, LANES))
    mask = mask_ref[...].astype(F32)
    last_pair = ra_ref.shape[1] - 1
    spread = []
    for y in range(-2, rows + 2):
        base = STRIP * (y + 2)
        hit = ((x_of == 0) & (lane_of == base + 3)) | ((x_of == LANES - 1) & (lane_of == base + 6))
        if 0 <= y < rows:
            line = mask[y : y + 1]
        else:
            j = halo_at(y, rows)
            line = jnp.where(
                row_odd == (y < 0), ra_ref[j, last_pair].astype(F32), rb_ref[j, last_pair].astype(F32)
            )[:1]
        emits = (lane_of >= spare) & (lane_of < spare + 3)
        table = jnp.where(hit, 1.0, jnp.where(emits, line, 0.0)).astype(BF16)
        spread.append(table)
    slot = 0
    slots = {}
    for step in range(STEPS):
        both = bound_ref[step]
        reach = STEPS - 1 - step
        for y in range(-reach, rows + reach, 2):
            pair = jnp.concatenate([spread[y + 2], spread[y + 3]], axis=1)
            got = jnp.dot(both, pair, preferred_element_type=F32)
            for side in range(2):
                slots[step, y + side] = slot
                source_ref[slot] = got[:, side * LANES : (side + 1) * LANES]
                slot += 1

    fall_ref[...] = jnp.zeros(fall_ref.shape, F32)
    unroll = 16
    skipped = slots[1, -1]

    def some_levels(trip, carry):
        ks = [trip * unroll + u for u in range(unroll)]
        coefs = [{} for _ in ks]
        states = [[{} for _ in range(STEPS + 1)] for _ in ks]
        for front in range(-2, rows + 4):
            for step in range(STEPS):
                y = front - step
                reach = STEPS - 1 - step
                if not -reach <= y < rows + reach:
                    continue
                index = slots[step, y]
                if step == 0:
                    for u, k in enumerate(ks):
                        at_k = pl.ds(k * bins, bins)
                        states[u][1][y] = part_ref[y + 2, at_k, :] + source_ref[index, at_k, :]
                    continue
                fall = fall_ref[index - skipped]
                for u, k in enumerate(ks):
                    if step == 1:
                        coefs[u][y] = [centre_ref[y + 1, pl.ds(k, bins, stride=0), :] - settle] + [
                            coef_ref[5 * (y + 2) + i, pl.ds(k, bins, stride=0), :] for i in range(1, 5)
                        ]
                    state = states[u][step]
                    c = coefs[u][y]
                    a = state[y]
                    source = source_ref[index, pl.ds(k * bins, bins), :] + fall
                    fall = settle * a
                    fresh = (
                        c[0] * a
                        + (c[1] * roll_lanes(a, 1) + c[2] * roll_lanes(a, -1))
                        + (c[3] * state[y - 1] + c[4] * state[y + 1])
                        + source
                    )
                    if step < STEPS - 1:
                        states[u][step + 1][y] = fresh
                    else:
                        out_ref[pl.ds(k * rows + y, bins, stride=stride), :] = fresh
                fall_ref[index - skipped] = fall
        return carry

    lax.fori_loop(0, levels // unroll, some_levels, 0)
    for y in range(rows):
        deposit_ref[pl.ds(y, bins, stride=rows), :] = (
            fallen_ref[y] + fall_ref[slots[1, y] - skipped] + fall_ref[slots[2, y] - skipped]
        )


def per_device(conc, nwp, lev_lo, frac, pick, corner_slot, corner_wt, settle, source_mask, profile):
    bins, levels, rows, cols = conc.shape
    peers = pick.shape[2]
    shape = jax.ShapeDtypeStruct
    flat = conc.reshape(bins * levels * rows, cols)

    sent = call(
        select_kernel,
        shape((peers, levels, LANES), BF16),
        (lev_lo.reshape(1, -1), frac.reshape(1, -1), pick.reshape(peers, -1), nwp),
        scratch=(
            pltpu.VMEM((peers, levels, LANES), BF16),
            pltpu.SemaphoreType.DMA((peers // 4,)),
        ),
        out_spaces=(pltpu.HBM,),
        flops=2 * 2 * levels * 2048 * 2048,
    )

    flat, sent = lax.optimization_barrier((flat, sent))
    received = lax.all_to_all(sent, "rows", split_axis=0, concat_axis=0, tiled=True)

    pairs = levels // 2 + 1
    edge_rows = shape((HALO, pairs, 2 * bins, cols), BF16)
    ca, cb = call(conc_edge_kernel, (edge_rows, edge_rows), (flat, source_mask), moved=0)
    ra, rb = swap(ca, "rows", True), swap(cb, "rows", False)

    wind_rows = shape((HALO, 2 * levels, cols), BF16)
    winds, wa, wb = call(
        horizontal_kernel,
        (shape((rows, 2 * levels, cols), F32), wind_rows, wind_rows),
        (received, corner_slot, corner_wt),
        scratch=(pltpu.VMEM((2 * levels, peers * LANES // 2), BF16),),
        flops=HIDES,
        limit=20,
    )
    wra, wrb = swap(wa, "rows", True), swap(wb, "rows", False)

    ra, rb, wa = lax.optimization_barrier((ra, rb, wa))
    strips = shape((pairs * 2 * bins, LANES), BF16)
    conc_strip = call(
        conc_strip_kernel, strips, (flat, source_mask, ra, rb),
        scratch=(pltpu.VMEM((2, pairs * 2 * bins, LANES), BF16),),
        moved=0,
    )
    own = call(
        side_strip_kernel,
        shape((pairs * 2 * bins + 2 * levels, LANES), BF16),
        (winds, wra, wrb, conc_strip),
        flops=HIDES,
    )
    xa, xb = swap(own, "cols", True), swap(own, "cols", False)

    tile = (bins, LANES)
    part, coef, fallen = (
        shape((rows + 4, levels * bins, LANES), F32),
        shape((5 * (rows + 4), levels, LANES), F32),
        shape((rows,) + tile, F32),
    )
    coef, part, fallen = call(
        first_step_kernel,
        (coef, part, fallen),
        (flat, settle, ra, rb, winds, wra, wrb),
        scratch=(pltpu.VMEM((rows + 4,) + tile, F32),),
        smem=(1,),
        moved=0,
    )
    updates = sum(rows + 2 * (STEPS - 1 - s) for s in range(STEPS))
    final, deposit = call(
        transport_kernel,
        (shape(flat.shape, F32), shape((bins * rows, cols), F32)),
        (part, coef, fallen, source_mask, settle, profile, ra, rb, own, xa, xb),
        scratch=(
            pltpu.VMEM((rows + 2, levels, LANES), F32),
            pltpu.VMEM((6, levels, LANES), F32),
            pltpu.VMEM((STEPS, levels * bins, LANES), BF16),
            pltpu.VMEM((updates, levels * bins, LANES), F32),
            pltpu.VMEM((updates - rows - 4,) + tile, F32),
        ),
        smem=(4,),
        flops=16 * updates * levels * bins * LANES,
        limit=24,
    )
    return final.reshape(conc.shape), deposit.reshape(bins, rows, cols)


def solution(mesh):
    placed = (
        P(None, None, "rows", "cols"),
        P(None, None, "rows"),
        P(),
        P(),
        P("rows", "cols", None, None),
        P(None, "rows", "cols"),
        P(None, "rows", "cols"),
        P(),
        P("rows", "cols"),
        P(),
    )
    return jax.shard_map(
        per_device,
        mesh=mesh,
        in_specs=placed,
        out_specs=(P(None, None, "rows", "cols"), P(None, "rows", "cols")),
        check_vma=False,
    )
```
